32 devices in a mesh: grp: 2 (over y), ctx: 4 (over z), sec: 2 (over core), tp: 2 (over x).
Axes of the slice: x: 2, y: 2, z: 4, core: 2. Of those that a mesh axis runs over, the one named last changes fastest.
Arguments:
- hidden: bfloat16 [1024, 8192], P(('grp', 'ctx', 'sec')), parts along dimension 0, may hold values from -6 to 6
- w_query: bfloat16 [2, 8192, 4096], P('sec', 'ctx', 'tp'), may hold values from -0.0625 to 0.0625
- key_projection: bfloat16 [2, 8192, 1024], P('sec', 'ctx', 'tp'), may hold values from -0.0625 to 0.0625
- value_projection: bfloat16 [2, 8192, 1024], P('sec', 'ctx', 'tp'), may hold values from -0.0625 to 0.0625
- score_head: bfloat16 [2, 4096], P('sec', 'tp'), may hold values from -0.09375 to 0.09375
- lengths: int32 [8], P('grp'), parts along dimension 0, may hold values from 1 to 320, 512 in all
- prompt_len: int32 [8], P('grp'), parts along dimension 0, may hold values from 1 to 159
- reward: float32 [8], P('grp'), parts along dimension 0, may hold values from -4 to 4
Outputs:
- kl_term: float32 [1024], P(('grp', 'ctx', 'sec')), parts along dimension 0
- objective: float32 [1024], P(('grp', 'ctx', 'sec')), parts along dimension 0
The draws below stay inside these ranges and needn't reach their ends.
There are 2 independent parts, one for each index of `grp`. The reference program is written for one: setup_inputs(seed, part) draws one part's arguments, and reference() takes and returns one part's arrays. A program takes and returns all parts, laid end to end along the dimension named above; an argument that names none is the same for every part. Nothing has to cross between parts.
Inputs may be any that keep to these rules, and one draw needn't show every extreme that they name: `lengths`: rollouts are packed in order and fill all 512 positions; the longest has exactly 320 tokens. `prompt_len`: A prompt may cover its whole rollout, leaving no response tokens.
All inputs are finite; a program needn't handle non-finite values.
Results may differ from the reference program's by a relative error of at most 0.012.
Values may be sent and summed in bfloat16 or wider, within the bound.
No kernel may reach another device: no remote copies, remote signals or barrier semaphores. Data moves between devices by JAX's collectives and lax.ppermute only.
A program may use at most 128 MiB of HBM per device.

```python
import math
import jax
import jax.numpy as jnp
import numpy as np
from jax import lax

MODEL_WIDTH = 8192
QUERY_HEAD_COUNT = 32
KEY_VALUE_HEADS = 8
HEAD_SIZE = 128
ROLLS = 4
TOKENS = 512
MOST = 320


def place_ends(entries, key, smallest, largest):
    place = [jax.random.randint(jax.random.fold_in(key, axis), (), 0, length) for axis, length in enumerate(entries.shape)]
    main_axis = entries.shape.index(max(entries.shape))
    beside = place[:main_axis] + [(place[main_axis] + 1) % entries.shape[main_axis]] + place[main_axis + 1:]
    return entries.at[tuple(place)].set(smallest).at[tuple(beside)].set(largest)


def block_levels(key, dims, split, low, top_value):
    factor_of, own = 1.0, jax.random.fold_in(key, 6)
    for axis_at, shards_of in split:
        heights = jnp.exp(jax.random.uniform(jax.random.fold_in(own, axis_at), (shards_of,), jnp.float32, low / len(split), top_value / len(split)))
        factor_of = factor_of * jnp.repeat(heights, dims[axis_at] // shards_of).reshape([-1 if axis == axis_at else 1 for axis in range(len(dims))])
    return factor_of


def length_profile(number_of, total, bound, slope):
    weights = [(1 << 20) // math.isqrt(standing ** slope) + 1 for standing in range(2, number_of + 1)]
    rest, given = total - bound - (number_of - 1), [1] * (number_of - 1)
    while rest > 0:
        movable = [i for i in range(number_of - 1) if given[i] < bound]
        mass, remaining = sum([weights[i] for i in movable]), rest
        for i in movable:
            more = min(bound - given[i], max(1, remaining * weights[i] // mass), rest)
            given[i] = given[i] + more
            rest = rest - more
    return np.array([bound] + given)


def ragged(rng, number_of, total, limit, lean):
    if number_of == 2:
        one = jax.random.randint(rng, (), max(1, total - limit), min(limit, total - 1) + 1)
        return jnp.stack([one, total - one])
    sizes = jnp.asarray(length_profile(number_of, total, limit, lean), jnp.int32)
    twos = (number_of - 1) // 2
    giver, taker = sizes[1:1 + 2 * twos:2], sizes[2:2 + 2 * twos:2]
    slack = jnp.minimum(giver - 1, limit - taker)
    passed = jax.random.randint(jax.random.fold_in(rng, 1), (twos,), 0, 1 << 20) % (slack + 1)
    sizes = sizes.at[1:1 + 2 * twos:2].set(giver - passed).at[2:2 + 2 * twos:2].set(taker + passed)
    return sizes[jax.random.permutation(jax.random.fold_in(rng, 2), number_of)]


def noise(stream_key, extent, scale, bound, cuts=(), kind=jnp.bfloat16):
    array = scale * jax.random.normal(stream_key, extent, jnp.float32)
    if cuts:
        array = array * block_levels(stream_key, extent, cuts, -0.22, 0.18)
    return jnp.clip(array, -bound, bound).astype(kind)


def setup_inputs(seed: int = 0, part: int = 0) -> dict:
    key_of = jax.random.split(jax.random.key(seed), 9)
    part_splits = jax.random.split(jax.random.fold_in(key_of[8], part), 9)
    hidden = noise(part_splits[0], (TOKENS, MODEL_WIDTH), 1.0, 6.0, ((0, 8),))
    w_query = noise(key_of[1], (2, MODEL_WIDTH, QUERY_HEAD_COUNT * HEAD_SIZE), MODEL_WIDTH ** -0.5, 0.0625, ((0, 2), (1, 4), (2, 2)))
    key_projection = noise(key_of[2], (2, MODEL_WIDTH, KEY_VALUE_HEADS * HEAD_SIZE), MODEL_WIDTH ** -0.5, 0.0625, ((0, 2), (1, 4), (2, 2)))
    value_projection = noise(key_of[3], (2, MODEL_WIDTH, KEY_VALUE_HEADS * HEAD_SIZE), MODEL_WIDTH ** -0.5, 0.0625, ((0, 2), (1, 4), (2, 2)))
    score_head = noise(key_of[4], (2, QUERY_HEAD_COUNT * HEAD_SIZE), (QUERY_HEAD_COUNT * HEAD_SIZE) ** -0.5, 0.09375, ((0, 2), (1, 2)))
    lengths = ragged(part_splits[5], ROLLS, TOKENS, MOST, 2).astype(jnp.int32)
    prompt_len = place_ends(jax.random.randint(part_splits[6], (ROLLS,), 1, MOST // 2), jax.random.fold_in(part_splits[6], 1), 1, (MOST // 2) - 1).astype(jnp.int32)
    reward = noise(part_splits[7], (ROLLS,), 1.0, 4.0, (), jnp.float32)
    return {"hidden": hidden, "w_query": w_query, "key_projection": key_projection, "value_projection": value_projection, "score_head": score_head, "lengths": lengths, "prompt_len": prompt_len, "reward": reward}


BETA = 0.1
NEGATIVE = -1e+30

def rollout_tables(lengths, prompt_len, reward, position):
    starts = (jnp.cumsum(lengths) - lengths).astype(jnp.int32)
    inside = starts[None, :] <= position[:, None]
    begin = lax.optimization_barrier(jnp.max(jnp.where(inside, starts[None, :], 0), axis=1)).astype(jnp.int32)
    latest = (lax.optimization_barrier(jnp.sum(inside.astype(jnp.int32), axis=1)) - 1).astype(jnp.int32)
    chosen = jnp.arange(lengths.shape[0], dtype=jnp.int32)[None, :] == latest[:, None]
    prompt = lax.optimization_barrier(jnp.sum(jnp.where(chosen, prompt_len[None, :], 0), axis=1)).astype(jnp.int32)
    centred = reward - jnp.mean(reward)
    advantage = lax.optimization_barrier(jnp.sum(jnp.where(chosen, centred[None, :], jnp.zeros_like(centred)[None, :]), axis=1))
    answer = (position - begin >= prompt).astype(reward.dtype)
    return (begin, answer, advantage)

def section_score(hidden, query_w, key_w, value_w, head_w, begin):
    packed_tokens = hidden.shape[0]
    query_group = QUERY_HEAD_COUNT // KEY_VALUE_HEADS
    query_rows = jnp.dot(hidden, query_w, preferred_element_type=jnp.float32).astype(jnp.bfloat16)
    key_rows = jnp.dot(hidden, key_w, preferred_element_type=jnp.float32).astype(jnp.bfloat16)
    value_rows = jnp.dot(hidden, value_w, preferred_element_type=jnp.float32).astype(jnp.bfloat16)
    query_rows = query_rows.reshape(packed_tokens, KEY_VALUE_HEADS, query_group, HEAD_SIZE).transpose(1, 0, 2, 3)
    key_rows = key_rows.reshape(packed_tokens, KEY_VALUE_HEADS, HEAD_SIZE).transpose(1, 0, 2)
    value_rows = value_rows.reshape(packed_tokens, KEY_VALUE_HEADS, HEAD_SIZE).transpose(1, 0, 2)
    block = math.gcd(packed_tokens, 512)
    position = jnp.arange(packed_tokens, dtype=jnp.int32)
    score_scale = HEAD_SIZE ** (-0.5)

    def one_head(operands):
        query_head, key_head, value_head = operands
        widened_key = key_head.astype(jnp.float32)
        widened_value = value_head.astype(jnp.float32)

        def one_block(first):
            token_rows = lax.dynamic_slice_in_dim(query_head, first, block, 0).astype(jnp.float32)
            row_pos = first + jnp.arange(block, dtype=jnp.int32)
            row_begin = lax.dynamic_slice_in_dim(begin, first, block, 0)
            score_logits = jnp.einsum('qsi,xi->sqx', token_rows, widened_key) * score_scale
            valid = (position[None, :] <= row_pos[:, None]) & (position[None, :] >= row_begin[:, None])
            peak = lax.optimization_barrier(jnp.max(jnp.where(valid[None], score_logits, NEGATIVE), axis=2, keepdims=True))
            weights = jnp.where(valid[None], jnp.exp(score_logits - peak), jnp.zeros_like(score_logits))
            rounded_scores = lax.optimization_barrier(weights.astype(jnp.bfloat16)).astype(jnp.float32)
            mixed_values = jnp.einsum('nih,hk->ink', rounded_scores, widened_value)
            total = lax.optimization_barrier(jnp.sum(weights, axis=2))
            return mixed_values / total.T[:, :, None]
        firsts = jnp.arange(packed_tokens // block, dtype=jnp.int32) * block
        return lax.map(one_block, firsts).reshape(packed_tokens, query_group, HEAD_SIZE)
    heads_out = lax.map(one_head, (query_rows, key_rows, value_rows))
    attended = heads_out.transpose(1, 0, 2, 3).reshape(packed_tokens, QUERY_HEAD_COUNT * HEAD_SIZE)
    head_wide = head_w.astype(jnp.float32)
    numerator = jnp.dot(attended, head_wide, precision=lax.Precision.HIGHEST)
    squares = lax.optimization_barrier(jnp.sum(attended * attended, axis=1))
    return numerator / jnp.sqrt(squares / (QUERY_HEAD_COUNT * HEAD_SIZE) + 1e-05)

def reference(hidden, w_query, key_projection, value_projection, score_head, lengths, prompt_len, reward):
    packed_tokens = hidden.shape[0]
    position = jnp.arange(packed_tokens, dtype=jnp.int32)
    begin, answer, advantage = rollout_tables(lengths, prompt_len, reward, position)
    policy = section_score(hidden, w_query[0], key_projection[0], value_projection[0], score_head[0], begin)
    frozen = section_score(hidden, w_query[1], key_projection[1], value_projection[1], score_head[1], begin)
    gap = frozen - policy
    kl_term = answer * (jnp.exp(gap) - gap - 1.0)
    objective = answer * advantage - BETA * kl_term
    return (kl_term, objective)
```

```python
import jax
import jax.numpy as jnp
from jax import lax
from jax.experimental import pallas as pl
from jax.experimental.pallas import tpu as pltpu
from jax.sharding import PartitionSpec as P

QUERY_HEAD_COUNT = 32
KEY_VALUE_HEADS = 8
HEAD_SIZE = 128


BETA = 0.1
NEGATIVE = -1e30
LINK_SCALE = 16.0
GROUP = QUERY_HEAD_COUNT // KEY_VALUE_HEADS


def swapped(array, axis, distance):
    return lax.ppermute(array, axis, [(i, i ^ 1 << distance) for i in range(lax.axis_size(axis))])


def rollout_tables(lengths, prompt_len, reward, position):
    starts = jnp.cumsum(lengths) - lengths
    inside = starts[None, :] <= position[:, None]
    begin = jnp.max(jnp.where(inside, starts[None, :], 0), axis=1)
    latest = jnp.sum(inside.astype(jnp.int32), axis=1) - 1
    chosen = jnp.arange(lengths.shape[0], dtype=jnp.int32)[None, :] == latest[:, None]
    prompt = jnp.sum(jnp.where(chosen, prompt_len[None, :], 0), axis=1)
    centred = reward - jnp.mean(reward)
    advantage = jnp.sum(
        jnp.where(chosen, centred[None, :], jnp.zeros_like(centred)[None, :]), axis=1
    )
    answer = (position - begin >= prompt).astype(reward.dtype)
    return (begin, answer, advantage)


def gathered_shards(
    hidden, w_query, key_projection, value_projection, score_head, lengths, prompt_len, reward
):
    row_block = lax.all_gather(hidden, "sec", axis=0, tiled=True)
    token_rows = row_block.shape[0]
    query_w = w_query[0]
    key_w = key_projection[0]
    value_w = value_projection[0]
    head_w = score_head[0]
    query_cols = query_w.shape[1]
    pair_cols = key_w.shape[1]

    def add_rows(piece):
        return jnp.dot(row_block, piece, preferred_element_type=jnp.float32)

    query_rows = add_rows(lax.all_gather(query_w, "ctx", axis=0, tiled=True))
    key_rows = add_rows(lax.all_gather(key_w, "ctx", axis=0, tiled=True))
    value_rows = add_rows(lax.all_gather(value_w, "ctx", axis=0, tiled=True))
    query_rows = query_rows.astype(jnp.bfloat16)
    key_rows = key_rows.astype(jnp.bfloat16)
    value_rows = value_rows.astype(jnp.bfloat16)
    heads_here = pair_cols // HEAD_SIZE
    score_scale = HEAD_SIZE ** (-0.5)
    row_pos = lax.axis_index("ctx") * token_rows + jnp.arange(token_rows, dtype=jnp.int32)
    begin, answer, advantage = rollout_tables(lengths, prompt_len, reward, row_pos)
    first_begin = jnp.min(begin)
    last_row = row_pos[token_rows - 1]
    query_heads = query_rows.reshape(token_rows, heads_here, GROUP, HEAD_SIZE)
    start_state = (
        jnp.full((heads_here, GROUP, token_rows), NEGATIVE, jnp.float32),
        jnp.zeros((heads_here, GROUP, token_rows), jnp.float32),
        jnp.zeros((heads_here, GROUP, token_rows, HEAD_SIZE), jnp.float32),
    )
    key_piece = lax.all_gather(key_rows, "ctx", axis=0, tiled=True)
    value_piece = lax.all_gather(value_rows, "ctx", axis=0, tiled=True)
    count = key_piece.shape[0] // token_rows

    def tile_step(index, carried):
        offset = index * token_rows
        key_tile = lax.dynamic_slice_in_dim(key_piece, offset, token_rows, 0).reshape(
            token_rows, heads_here, HEAD_SIZE
        )
        value_tile = lax.dynamic_slice_in_dim(value_piece, offset, token_rows, 0).reshape(
            token_rows, heads_here, HEAD_SIZE
        )
        key_pos = offset + jnp.arange(token_rows, dtype=jnp.int32)

        def update(current):
            peak, weight_sum, mixed_values = current
            score_logits = (
                jnp.einsum(
                    "rkgd,pkd->kgrp", query_heads, key_tile, preferred_element_type=jnp.float32
                )
                * score_scale
            )
            valid = (key_pos[None, :] <= row_pos[:, None]) & (key_pos[None, :] >= begin[:, None])
            masked = jnp.where(valid[None, None], score_logits, NEGATIVE)
            new_peak = jnp.maximum(peak, jnp.max(masked, axis=3))
            weights = jnp.where(
                valid[None, None],
                jnp.exp(score_logits - new_peak[..., None]),
                jnp.zeros_like(score_logits),
            )
            factor = jnp.exp(peak - new_peak)
            new_sum = weight_sum * factor + jnp.sum(weights, axis=3)
            product = jnp.einsum(
                "kgrp,pkd->kgrd",
                weights.astype(jnp.bfloat16),
                value_tile,
                preferred_element_type=jnp.float32,
            )
            return (new_peak, new_sum, mixed_values * factor[..., None] + product)

        live = (offset <= last_row) & (offset + token_rows - 1 >= first_begin)
        return lax.cond(live, update, lambda kept: kept, carried)

    peak, weight_sum, mixed_values = lax.fori_loop(0, count, tile_step, start_state)
    attended = (
        (mixed_values / weight_sum[..., None]).transpose(2, 0, 1, 3).reshape(token_rows, query_cols)
    )
    numerator = jnp.dot(attended, head_w.astype(jnp.float32), precision=lax.Precision.HIGHEST)
    squares = jnp.sum(attended * attended, axis=1)
    section = lax.axis_index("sec")
    total_num, total_sq = lax.psum((numerator, squares), "tp")
    score = total_num / jnp.sqrt(total_sq / (QUERY_HEAD_COUNT * HEAD_SIZE) + 1e-05)
    other = swapped(score, "sec", 0)
    policy = jnp.where(section == 0, score, other)
    frozen = jnp.where(section == 0, other, score)
    gap = frozen - policy
    kl_full = answer * (jnp.exp(gap) - gap - 1.0)
    objective_full = answer * advantage - BETA * kl_full
    half = token_rows // 2
    kl_term = lax.dynamic_slice_in_dim(kl_full, section * half, half, 0)
    objective = lax.dynamic_slice_in_dim(objective_full, section * half, half, 0)
    return (kl_term, objective)


def attention_kernel(lengths, section, block, head, out, rows):
    tokens = block.shape[0]
    flip = section[0] * rows

    def place(shape, axis):
        return lax.broadcasted_iota(jnp.int32, shape, axis) ^ flip

    query_pos = place((1, tokens), 1)
    begin = jnp.zeros((1, tokens), jnp.int32)
    start = jnp.int32(0)
    for index in range(lengths.shape[0] - 1):
        start = start + lengths[index]
        begin = jnp.where(query_pos >= start, start, begin)
    key_pos = place((tokens, 1), 0)
    valid = (key_pos <= query_pos) & (key_pos >= begin)
    wide = GROUP * HEAD_SIZE
    key = block[:, wide : wide + HEAD_SIZE]
    value = block[:, wide + HEAD_SIZE :]
    numerator = jnp.zeros((1, tokens), jnp.float32)
    squares = jnp.zeros((1, tokens), jnp.float32)
    for index in range(GROUP):
        cols = slice(index * HEAD_SIZE, (index + 1) * HEAD_SIZE)
        logits = lax.dot_general(
            key, block[:, cols], (((1,), (1,)), ((), ())), preferred_element_type=jnp.float32
        ) * (HEAD_SIZE ** (-0.5))
        masked = jnp.where(valid, logits, NEGATIVE)
        peak = jnp.max(masked, axis=0, keepdims=True)
        weights = jnp.exp(masked - peak)
        total = jnp.sum(weights, axis=0, keepdims=True)
        mixed = lax.dot_general(
            value,
            weights.astype(jnp.bfloat16),
            (((0,), (0,)), ((), ())),
            preferred_element_type=jnp.float32,
        )
        attended = mixed / total
        numerator += jnp.sum(attended * head[cols, :], axis=0, keepdims=True)
        squares += jnp.sum(attended * attended, axis=0, keepdims=True)
    out[0:1, :] = numerator
    out[1:2, :] = squares


def split_shards(
    hidden, w_query, key_projection, value_projection, score_head, lengths, prompt_len, reward
):
    rows = hidden.shape[0]
    depth = w_query.shape[1]
    ctx = lax.axis_index("ctx")
    section = lax.axis_index("sec")
    count = 4
    f16, f32 = jnp.float16, jnp.float32

    def columns(target):
        return lax.dynamic_slice_in_dim(hidden, (target % count) * depth, depth, 1)

    pieces = {0: columns(ctx)}
    for step in (2, 1, 3):
        pairs = [(i, (i + step) % count) for i in range(count)]
        pieces[step] = lax.ppermute(columns(ctx + step), "ctx", pairs)
    both = {
        step: jnp.concatenate([piece, swapped(piece, "sec", 0)], axis=0)
        for step, piece in pieces.items()
    }
    ring = jnp.concatenate([both[3], both[2], both[1], both[0]], axis=0)
    doubled = jnp.concatenate([ring, ring], axis=0)
    chip_rows = 2 * rows
    tokens_by_ctx = lax.dynamic_slice_in_dim(
        doubled, ((count - 1 - ctx) % count) * chip_rows, count * chip_rows, 0
    )

    def product(weight):
        total = jnp.dot(tokens_by_ctx, weight, preferred_element_type=f32)
        return (total * LINK_SCALE).astype(f16)

    query_part = product(w_query[0])
    key_part = product(key_projection[0])
    value_part = product(value_projection[0])
    wide = GROUP * HEAD_SIZE

    def block(owner):
        return jnp.concatenate(
            [
                lax.dynamic_slice_in_dim(query_part, owner * wide, wide, 1),
                lax.dynamic_slice_in_dim(key_part, owner * HEAD_SIZE, HEAD_SIZE, 1),
                lax.dynamic_slice_in_dim(value_part, owner * HEAD_SIZE, HEAD_SIZE, 1),
            ],
            axis=1,
        )

    left = ctx < 2
    far = block(jnp.where(left, 3, 0))
    fold = lax.ppermute(far, "ctx", [(0, 1), (3, 2)])
    middle = lax.ppermute(block(3 - ctx), "ctx", [(1, 2), (2, 1)])
    skip = lax.ppermute(block(jnp.where(left, 2, 1)), "ctx", [(0, 2), (3, 1)])
    near = lax.ppermute(block(ctx ^ 1), "ctx", [(0, 1), (1, 0), (2, 3), (3, 2)])
    folded = (far.astype(f32) + fold.astype(f32)).astype(f16)
    ends = lax.ppermute(folded, "ctx", [(1, 3), (2, 0)])
    total = block(ctx).astype(f32)
    for part in (middle, skip, near, ends):
        total = total + part.astype(f32)
    mine = (total * (1.0 / LINK_SCALE)).astype(jnp.bfloat16)

    head = lax.dynamic_slice_in_dim(score_head[0], ctx * wide, wide, 0).astype(f32)
    tokens = mine.shape[0]
    sums = pl.pallas_call(
        lambda *refs: attention_kernel(*refs, rows),
        out_shape=jax.ShapeDtypeStruct((2, tokens), f32),
        in_specs=[
            pl.BlockSpec(memory_space=pltpu.SMEM),
            pl.BlockSpec(memory_space=pltpu.SMEM),
            pl.BlockSpec(memory_space=pltpu.VMEM),
            pl.BlockSpec(memory_space=pltpu.VMEM),
        ],
        out_specs=pl.BlockSpec(memory_space=pltpu.VMEM),
        compiler_params=pltpu.CompilerParams(vmem_limit_bytes=32 * 1024 * 1024),
    )(lengths, section.reshape(1), mine, head.reshape(wide, 1))

    spread = sums.reshape(2, count, 2, rows)
    spread = jnp.where(section == 0, spread, jnp.flip(spread, axis=2))
    spread = jnp.broadcast_to(
        spread.transpose(1, 2, 0, 3)[:, :, None], (count, 2, 2, 2, rows)
    ).reshape(count * 4, 2, rows)
    spread = lax.all_to_all(spread, ("ctx", "sec", "tp"), 0, 0, tiled=True)
    spread = jnp.sum(spread.reshape(count, 2, 2, 2, rows), axis=(0, 2))
    scores = spread[:, 0] / jnp.sqrt(spread[:, 1] / (QUERY_HEAD_COUNT * HEAD_SIZE) + 1e-05)
    position = (ctx * 2 + section) * rows + jnp.arange(rows, dtype=jnp.int32)
    _, answer, advantage = rollout_tables(lengths, prompt_len, reward, position)
    gap = scores[1] - scores[0]
    kl_term = answer * (jnp.exp(gap) - gap - 1.0)
    objective = answer * advantage - BETA * kl_term
    return (kl_term, objective)


def solution(mesh):
    placed = (
        P(("grp", "ctx", "sec"), None),
        P("sec", "ctx", "tp"),
        P("sec", "ctx", "tp"),
        P("sec", "ctx", "tp"),
        P("sec", "tp"),
        P("grp"),
        P("grp"),
        P("grp"),
    )
    own_heads = KEY_VALUE_HEADS // mesh.shape["tp"]
    by_heads = mesh.shape["ctx"] == 4 and own_heads == 4
    return jax.shard_map(
        split_shards if by_heads else gathered_shards,
        mesh=mesh,
        in_specs=placed,
        out_specs=(P(("grp", "ctx", "sec")), P(("grp", "ctx", "sec"))),
        check_vma=False,
    )
```

```python
import jax
import jax.numpy as jnp
from jax import lax
from jax.experimental import pallas as pl
from jax.experimental.pallas import tpu as pltpu
from jax.sharding import PartitionSpec as P

QUERY_HEAD_COUNT = 32
KEY_VALUE_HEADS = 8
HEAD_SIZE = 128


BETA = 0.1
NEGATIVE = -1e30
LINK_SCALE = 16.0
GROUP = QUERY_HEAD_COUNT // KEY_VALUE_HEADS


def swapped(array, axis, distance):
    return lax.ppermute(array, axis, [(i, i ^ 1 << distance) for i in range(lax.axis_size(axis))])


def rollout_tables(lengths, prompt_len, reward, position):
    starts = jnp.cumsum(lengths) - lengths
    inside = starts[None, :] <= position[:, None]
    begin = jnp.max(jnp.where(inside, starts[None, :], 0), axis=1)
    latest = jnp.sum(inside.astype(jnp.int32), axis=1) - 1
    chosen = jnp.arange(lengths.shape[0], dtype=jnp.int32)[None, :] == latest[:, None]
    prompt = jnp.sum(jnp.where(chosen, prompt_len[None, :], 0), axis=1)
    centred = reward - jnp.mean(reward)
    advantage = jnp.sum(
        jnp.where(chosen, centred[None, :], jnp.zeros_like(centred)[None, :]), axis=1
    )
    answer = (position - begin >= prompt).astype(reward.dtype)
    return (begin, answer, advantage)


def gathered_shards(
    hidden, w_query, key_projection, value_projection, score_head, lengths, prompt_len, reward
):
    row_block = lax.all_gather(hidden, "sec", axis=0, tiled=True)
    token_rows = row_block.shape[0]
    query_w = w_query[0]
    key_w = key_projection[0]
    value_w = value_projection[0]
    head_w = score_head[0]
    query_cols = query_w.shape[1]
    pair_cols = key_w.shape[1]

    def add_rows(piece):
        return jnp.dot(row_block, piece, preferred_element_type=jnp.float32)

    query_rows = add_rows(lax.all_gather(query_w, "ctx", axis=0, tiled=True))
    key_rows = add_rows(lax.all_gather(key_w, "ctx", axis=0, tiled=True))
    value_rows = add_rows(lax.all_gather(value_w, "ctx", axis=0, tiled=True))
    query_rows = query_rows.astype(jnp.bfloat16)
    key_rows = key_rows.astype(jnp.bfloat16)
    value_rows = value_rows.astype(jnp.bfloat16)
    heads_here = pair_cols // HEAD_SIZE
    score_scale = HEAD_SIZE ** (-0.5)
    row_pos = lax.axis_index("ctx") * token_rows + jnp.arange(token_rows, dtype=jnp.int32)
    begin, answer, advantage = rollout_tables(lengths, prompt_len, reward, row_pos)
    first_begin = jnp.min(begin)
    last_row = row_pos[token_rows - 1]
    query_heads = query_rows.reshape(token_rows, heads_here, GROUP, HEAD_SIZE)
    start_state = (
        jnp.full((heads_here, GROUP, token_rows), NEGATIVE, jnp.float32),
        jnp.zeros((heads_here, GROUP, token_rows), jnp.float32),
        jnp.zeros((heads_here, GROUP, token_rows, HEAD_SIZE), jnp.float32),
    )
    key_piece = lax.all_gather(key_rows, "ctx", axis=0, tiled=True)
    value_piece = lax.all_gather(value_rows, "ctx", axis=0, tiled=True)
    count = key_piece.shape[0] // token_rows

    def tile_step(index, carried):
        offset = index * token_rows
        key_tile = lax.dynamic_slice_in_dim(key_piece, offset, token_rows, 0).reshape(
            token_rows, heads_here, HEAD_SIZE
        )
        value_tile = lax.dynamic_slice_in_dim(value_piece, offset, token_rows, 0).reshape(
            token_rows, heads_here, HEAD_SIZE
        )
        key_pos = offset + jnp.arange(token_rows, dtype=jnp.int32)

        def update(current):
            peak, weight_sum, mixed_values = current
            score_logits = (
                jnp.einsum(
                    "rkgd,pkd->kgrp", query_heads, key_tile, preferred_element_type=jnp.float32
                )
                * score_scale
            )
            valid = (key_pos[None, :] <= row_pos[:, None]) & (key_pos[None, :] >= begin[:, None])
            masked = jnp.where(valid[None, None], score_logits, NEGATIVE)
            new_peak = jnp.maximum(peak, jnp.max(masked, axis=3))
            weights = jnp.where(
                valid[None, None],
                jnp.exp(score_logits - new_peak[..., None]),
                jnp.zeros_like(score_logits),
            )
            factor = jnp.exp(peak - new_peak)
            new_sum = weight_sum * factor + jnp.sum(weights, axis=3)
            product = jnp.einsum(
                "kgrp,pkd->kgrd",
                weights.astype(jnp.bfloat16),
                value_tile,
                preferred_element_type=jnp.float32,
            )
            return (new_peak, new_sum, mixed_values * factor[..., None] + product)

        live = (offset <= last_row) & (offset + token_rows - 1 >= first_begin)
        return lax.cond(live, update, lambda kept: kept, carried)

    peak, weight_sum, mixed_values = lax.fori_loop(0, count, tile_step, start_state)
    attended = (
        (mixed_values / weight_sum[..., None]).transpose(2, 0, 1, 3).reshape(token_rows, query_cols)
    )
    numerator = jnp.dot(attended, head_w.astype(jnp.float32), precision=lax.Precision.HIGHEST)
    squares = jnp.sum(attended * attended, axis=1)
    section = lax.axis_index("sec")
    total_num, total_sq = lax.psum((numerator, squares), "tp")
    score = total_num / jnp.sqrt(total_sq / (QUERY_HEAD_COUNT * HEAD_SIZE) + 1e-05)
    other = swapped(score, "sec", 0)
    policy = jnp.where(section == 0, score, other)
    frozen = jnp.where(section == 0, other, score)
    gap = frozen - policy
    kl_full = answer * (jnp.exp(gap) - gap - 1.0)
    objective_full = answer * advantage - BETA * kl_full
    half = token_rows // 2
    kl_term = lax.dynamic_slice_in_dim(kl_full, section * half, half, 0)
    objective = lax.dynamic_slice_in_dim(objective_full, section * half, half, 0)
    return (kl_term, objective)


def attention_kernel(lengths, section, block, head, out, rows):
    tokens = block.shape[0]
    flip = section[0] * rows

    def place(shape, axis):
        return lax.broadcasted_iota(jnp.int32, shape, axis) ^ flip

    query_pos = place((1, tokens), 1)
    begin = jnp.zeros((1, tokens), jnp.int32)
    start = jnp.int32(0)
    for index in range(lengths.shape[0] - 1):
        start = start + lengths[index]
        begin = jnp.where(query_pos >= start, start, begin)
    key_pos = place((tokens, 1), 0)
    valid = (key_pos <= query_pos) & (key_pos >= begin)
    wide = GROUP * HEAD_SIZE
    key = block[:, wide : wide + HEAD_SIZE]
    value = block[:, wide + HEAD_SIZE :]
    numerator = jnp.zeros((1, tokens), jnp.float32)
    squares = jnp.zeros((1, tokens), jnp.float32)
    for index in range(GROUP):
        cols = slice(index * HEAD_SIZE, (index + 1) * HEAD_SIZE)
        logits = lax.dot_general(
            key, block[:, cols], (((1,), (1,)), ((), ())), preferred_element_type=jnp.float32
        ) * (HEAD_SIZE ** (-0.5))
        masked = jnp.where(valid, logits, NEGATIVE)
        peak = jnp.max(masked, axis=0, keepdims=True)
        weights = jnp.exp(masked - peak)
        total = jnp.sum(weights, axis=0, keepdims=True)
        mixed = lax.dot_general(
            value,
            weights.astype(jnp.bfloat16),
            (((0,), (0,)), ((), ())),
            preferred_element_type=jnp.float32,
        )
        attended = mixed / total
        numerator += jnp.sum(attended * head[cols, :], axis=0, keepdims=True)
        squares += jnp.sum(attended * attended, axis=0, keepdims=True)
    out[0:1, :] = numerator
    out[1:2, :] = squares


def partial_kernel(plan, *refs):
    pieces, (query_w, key_w, value_w, out, tokens) = refs[:8], refs[8:]
    rows = pieces[0].shape[0]
    wide = query_w.shape[2]

    @pl.when(pl.program_id(0) == 0)
    def _():
        for index, piece in enumerate(pieces):
            base = plan[index // 2] * (2 * rows) + (index % 2) * rows
            tokens[pl.ds(pl.multiple_of(base, rows), rows), :] = piece[...]

    step = 2 * rows
    for first in range(0, tokens.shape[0], step):
        held = tokens[first : first + step, :]
        for weight, start in ((query_w, 0), (key_w, wide), (value_w, wide + HEAD_SIZE)):
            total = jnp.dot(held, weight[0], preferred_element_type=jnp.float32)
            out[0, first : first + step, start : start + weight.shape[2]] = total * LINK_SCALE


def partials(plan, pieces, weights, skipped, count):
    rows, depth = pieces[0].shape
    wide = GROUP * HEAD_SIZE
    tokens = len(pieces) * rows
    cols = wide + 2 * HEAD_SIZE
    sources = len(pieces) // 2

    def owner_block(width):
        return pl.BlockSpec(
            (1, depth, width), lambda i, plan: (0, 0, plan[sources + skipped + i])
        )

    return pl.pallas_call(
        partial_kernel,
        out_shape=jax.ShapeDtypeStruct((count, tokens, cols), jnp.float32),
        grid_spec=pltpu.PrefetchScalarGridSpec(
            num_scalar_prefetch=1,
            grid=(count,),
            in_specs=[pl.BlockSpec((rows, depth), lambda i, plan: (0, 0)) for _ in pieces]
            + [owner_block(wide), owner_block(HEAD_SIZE), owner_block(HEAD_SIZE)],
            out_specs=pl.BlockSpec((1, tokens, cols), lambda i, plan: (i, 0, 0)),
            scratch_shapes=[pltpu.VMEM((tokens, depth), jnp.bfloat16)],
        ),
        compiler_params=pltpu.CompilerParams(vmem_limit_bytes=40 * 1024 * 1024),
        cost_estimate=pl.CostEstimate(
            flops=2 * count * tokens * depth * cols,
            bytes_accessed=2 * tokens * depth + count * cols * (2 * depth + 4 * tokens),
            transcendentals=0,
        ),
    )(plan, *pieces, *weights)


def split_shards(
    hidden, w_query, key_projection, value_projection, score_head, lengths, prompt_len, reward
):
    rows = hidden.shape[0]
    depth = w_query.shape[1]
    ctx = lax.axis_index("ctx")
    section = lax.axis_index("sec")
    count = 4
    f16, f32 = jnp.float16, jnp.float32

    def columns(target):
        return lax.dynamic_slice_in_dim(hidden, (target % count) * depth, depth, 1)

    order = (2, 1, 3, 0)
    pieces = []
    for step in order:
        pairs = [(i, (i + step) % count) for i in range(count)]
        piece = columns(ctx + step)
        if step:
            piece = lax.ppermute(piece, "ctx", pairs)
        pieces += [piece, swapped(piece, "sec", 0)]

    left = ctx < 2
    owners = (jnp.where(left, 3, 0), jnp.where(left, 2, 1), ctx ^ 1, ctx)
    plan = jnp.stack([(ctx - step) % count for step in order] + list(owners)).astype(jnp.int32)
    weights = (w_query, key_projection, value_projection)
    first = partials(plan, pieces, weights, 0, 2)
    second = partials(plan, pieces, weights, 2, 2)

    fold = lax.ppermute(first[0].astype(f16), "ctx", [(0, 1), (3, 2)])
    inner = first[1].astype(f16)
    middle = lax.ppermute(inner, "ctx", [(1, 2), (2, 1)])
    skip = lax.ppermute(inner, "ctx", [(0, 2), (3, 1)])
    near = lax.ppermute(second[0].astype(f16), "ctx", [(0, 1), (1, 0), (2, 3), (3, 2)])
    folded = (first[0] + fold.astype(f32)).astype(f16)
    ends = lax.ppermute(folded, "ctx", [(1, 3), (2, 0)])
    total = second[1]
    for part in (middle, skip, near, ends):
        total = total + part.astype(f32)
    mine = (total * (1.0 / LINK_SCALE)).astype(jnp.bfloat16)

    wide = GROUP * HEAD_SIZE
    head = lax.dynamic_slice_in_dim(score_head[0], ctx * wide, wide, 0).astype(f32)
    tokens = mine.shape[0]
    sums = pl.pallas_call(
        lambda *refs: attention_kernel(*refs, rows),
        out_shape=jax.ShapeDtypeStruct((2, tokens), f32),
        in_specs=[
            pl.BlockSpec(memory_space=pltpu.SMEM),
            pl.BlockSpec(memory_space=pltpu.SMEM),
            pl.BlockSpec(memory_space=pltpu.VMEM),
            pl.BlockSpec(memory_space=pltpu.VMEM),
        ],
        out_specs=pl.BlockSpec(memory_space=pltpu.VMEM),
        compiler_params=pltpu.CompilerParams(vmem_limit_bytes=32 * 1024 * 1024),
    )(lengths, section.reshape(1), mine, head.reshape(wide, 1))

    spread = sums.reshape(2, count, 2, rows)
    spread = jnp.where(section == 0, spread, jnp.flip(spread, axis=2))
    spread = jnp.broadcast_to(
        spread.transpose(1, 2, 0, 3)[:, :, None], (count, 2, 2, 2, rows)
    ).reshape(count * 4, 2, rows)
    spread = lax.all_to_all(spread, ("ctx", "sec", "tp"), 0, 0, tiled=True)
    spread = jnp.sum(spread.reshape(count, 2, 2, 2, rows), axis=(0, 2))
    scores = spread[:, 0] / jnp.sqrt(spread[:, 1] / (QUERY_HEAD_COUNT * HEAD_SIZE) + 1e-05)
    position = (ctx * 2 + section) * rows + jnp.arange(rows, dtype=jnp.int32)
    _, answer, advantage = rollout_tables(lengths, prompt_len, reward, position)
    gap = scores[1] - scores[0]
    kl_term = answer * (jnp.exp(gap) - gap - 1.0)
    objective = answer * advantage - BETA * kl_term
    return (kl_term, objective)


def solution(mesh):
    placed = (
        P(("grp", "ctx", "sec"), None),
        P("sec", "ctx", "tp"),
        P("sec", "ctx", "tp"),
        P("sec", "ctx", "tp"),
        P("sec", "tp"),
        P("grp"),
        P("grp"),
        P("grp"),
    )
    own_heads = KEY_VALUE_HEADS // mesh.shape["tp"]
    by_heads = mesh.shape["ctx"] == 4 and own_heads == 4
    return jax.shard_map(
        split_shards if by_heads else gathered_shards,
        mesh=mesh,
        in_specs=placed,
        out_specs=(P(("grp", "ctx", "sec")), P(("grp", "ctx", "sec"))),
        check_vma=False,
    )
```

```python
import jax
import jax.numpy as jnp
from jax import lax
from jax.experimental import pallas as pl
from jax.experimental.pallas import tpu as pltpu
from jax.sharding import PartitionSpec as P

QUERY_HEAD_COUNT = 32
KEY_VALUE_HEADS = 8
HEAD_SIZE = 128


BETA = 0.1
NEGATIVE = -1e30
LINK_SCALE = 16.0
GROUP = QUERY_HEAD_COUNT // KEY_VALUE_HEADS
GRANT = 12
PRICE = 1.0


def swapped(array, axis, distance):
    return lax.ppermute(array, axis, [(i, i ^ 1 << distance) for i in range(lax.axis_size(axis))])


def rollout_tables(lengths, prompt_len, reward, position):
    starts = jnp.cumsum(lengths) - lengths
    inside = starts[None, :] <= position[:, None]
    begin = jnp.max(jnp.where(inside, starts[None, :], 0), axis=1)
    latest = jnp.sum(inside.astype(jnp.int32), axis=1) - 1
    chosen = jnp.arange(lengths.shape[0], dtype=jnp.int32)[None, :] == latest[:, None]
    prompt = jnp.sum(jnp.where(chosen, prompt_len[None, :], 0), axis=1)
    centred = reward - jnp.mean(reward)
    advantage = jnp.sum(
        jnp.where(chosen, centred[None, :], jnp.zeros_like(centred)[None, :]), axis=1
    )
    answer = (position - begin >= prompt).astype(reward.dtype)
    return (begin, answer, advantage)


def gathered_shards(
    hidden, w_query, key_projection, value_projection, score_head, lengths, prompt_len, reward
):
    row_block = lax.all_gather(hidden, "sec", axis=0, tiled=True)
    token_rows = row_block.shape[0]
    query_w = w_query[0]
    key_w = key_projection[0]
    value_w = value_projection[0]
    head_w = score_head[0]
    query_cols = query_w.shape[1]
    pair_cols = key_w.shape[1]

    def add_rows(piece):
        return jnp.dot(row_block, piece, preferred_element_type=jnp.float32)

    query_rows = add_rows(lax.all_gather(query_w, "ctx", axis=0, tiled=True))
    key_rows = add_rows(lax.all_gather(key_w, "ctx", axis=0, tiled=True))
    value_rows = add_rows(lax.all_gather(value_w, "ctx", axis=0, tiled=True))
    query_rows = query_rows.astype(jnp.bfloat16)
    key_rows = key_rows.astype(jnp.bfloat16)
    value_rows = value_rows.astype(jnp.bfloat16)
    heads_here = pair_cols // HEAD_SIZE
    score_scale = HEAD_SIZE ** (-0.5)
    row_pos = lax.axis_index("ctx") * token_rows + jnp.arange(token_rows, dtype=jnp.int32)
    begin, answer, advantage = rollout_tables(lengths, prompt_len, reward, row_pos)
    first_begin = jnp.min(begin)
    last_row = row_pos[token_rows - 1]
    query_heads = query_rows.reshape(token_rows, heads_here, GROUP, HEAD_SIZE)
    start_state = (
        jnp.full((heads_here, GROUP, token_rows), NEGATIVE, jnp.float32),
        jnp.zeros((heads_here, GROUP, token_rows), jnp.float32),
        jnp.zeros((heads_here, GROUP, token_rows, HEAD_SIZE), jnp.float32),
    )
    key_piece = lax.all_gather(key_rows, "ctx", axis=0, tiled=True)
    value_piece = lax.all_gather(value_rows, "ctx", axis=0, tiled=True)
    count = key_piece.shape[0] // token_rows

    def tile_step(index, carried):
        offset = index * token_rows
        key_tile = lax.dynamic_slice_in_dim(key_piece, offset, token_rows, 0).reshape(
            token_rows, heads_here, HEAD_SIZE
        )
        value_tile = lax.dynamic_slice_in_dim(value_piece, offset, token_rows, 0).reshape(
            token_rows, heads_here, HEAD_SIZE
        )
        key_pos = offset + jnp.arange(token_rows, dtype=jnp.int32)

        def update(current):
            peak, weight_sum, mixed_values = current
            score_logits = (
                jnp.einsum(
                    "rkgd,pkd->kgrp", query_heads, key_tile, preferred_element_type=jnp.float32
                )
                * score_scale
            )
            valid = (key_pos[None, :] <= row_pos[:, None]) & (key_pos[None, :] >= begin[:, None])
            masked = jnp.where(valid[None, None], score_logits, NEGATIVE)
            new_peak = jnp.maximum(peak, jnp.max(masked, axis=3))
            weights = jnp.where(
                valid[None, None],
                jnp.exp(score_logits - new_peak[..., None]),
                jnp.zeros_like(score_logits),
            )
            factor = jnp.exp(peak - new_peak)
            new_sum = weight_sum * factor + jnp.sum(weights, axis=3)
            product = jnp.einsum(
                "kgrp,pkd->kgrd",
                weights.astype(jnp.bfloat16),
                value_tile,
                preferred_element_type=jnp.float32,
            )
            return (new_peak, new_sum, mixed_values * factor[..., None] + product)

        live = (offset <= last_row) & (offset + token_rows - 1 >= first_begin)
        return lax.cond(live, update, lambda kept: kept, carried)

    peak, weight_sum, mixed_values = lax.fori_loop(0, count, tile_step, start_state)
    attended = (
        (mixed_values / weight_sum[..., None]).transpose(2, 0, 1, 3).reshape(token_rows, query_cols)
    )
    numerator = jnp.dot(attended, head_w.astype(jnp.float32), precision=lax.Precision.HIGHEST)
    squares = jnp.sum(attended * attended, axis=1)
    section = lax.axis_index("sec")
    total_num, total_sq = lax.psum((numerator, squares), "tp")
    score = total_num / jnp.sqrt(total_sq / (QUERY_HEAD_COUNT * HEAD_SIZE) + 1e-05)
    other = swapped(score, "sec", 0)
    policy = jnp.where(section == 0, score, other)
    frozen = jnp.where(section == 0, other, score)
    gap = frozen - policy
    kl_full = answer * (jnp.exp(gap) - gap - 1.0)
    objective_full = answer * advantage - BETA * kl_full
    half = token_rows // 2
    kl_term = lax.dynamic_slice_in_dim(kl_full, section * half, half, 0)
    objective = lax.dynamic_slice_in_dim(objective_full, section * half, half, 0)
    return (kl_term, objective)


def token_places(index, section, rows):
    chip = 2 * rows
    row = lax.rem(index, chip)
    return index - row + lax.rem(row + section * rows, chip)


def attention_kernel(lengths, where, block, head, out, rows):
    tokens = block.shape[0]
    section = where[0]

    def place(shape, axis):
        return token_places(lax.broadcasted_iota(jnp.int32, shape, axis), section, rows)

    query_pos = place((1, tokens), 1)
    begin = jnp.zeros((1, tokens), jnp.int32)
    start = jnp.int32(0)
    for index in range(lengths.shape[0] - 1):
        start = start + lengths[index]
        begin = jnp.where(query_pos >= start, start, begin)
    key_pos = place((tokens, 1), 0)
    valid = (key_pos <= query_pos) & (key_pos >= begin)
    wide = GROUP * HEAD_SIZE
    key = block[:, wide : wide + HEAD_SIZE]
    value = block[:, wide + HEAD_SIZE :]
    numerator = jnp.zeros((1, tokens), jnp.float32)
    squares = jnp.zeros((1, tokens), jnp.float32)
    for index in range(GROUP):
        cols = slice(index * HEAD_SIZE, (index + 1) * HEAD_SIZE)
        logits = lax.dot_general(
            key, block[:, cols], (((1,), (1,)), ((), ())), preferred_element_type=jnp.float32
        ) * (HEAD_SIZE ** (-0.5))
        masked = jnp.where(valid, logits, NEGATIVE)
        peak = jnp.max(masked, axis=0, keepdims=True)
        weights = jnp.exp(masked - peak)
        total = jnp.sum(weights, axis=0, keepdims=True)
        mixed = lax.dot_general(
            value,
            weights.astype(jnp.bfloat16),
            (((0,), (0,)), ((), ())),
            preferred_element_type=jnp.float32,
        )
        attended = mixed / total
        column = jnp.broadcast_to(head[:, cols].astype(jnp.float32), (HEAD_SIZE, HEAD_SIZE)).T
        numerator += jnp.sum(attended * column[:, :1], axis=0, keepdims=True)
        squares += jnp.sum(attended * attended, axis=0, keepdims=True)
    for ctx in range(tokens // (2 * rows)):
        own = slice(2 * ctx * rows, (2 * ctx + 1) * rows)
        other = slice((2 * ctx + 1) * rows, (2 * ctx + 2) * rows)
        same, cross = (
            jnp.concatenate([numerator[:, part], squares[:, part]], axis=1)
            for part in (own, other)
        )
        for core in range(2):
            row = jnp.where(section == core, same, cross)
            for share in range(2):
                out[ctx * 4 + core * 2 + share] = row


def final_kernel(lengths, prompt_len, reward, where, parts, kl_term, objective):
    rows = kl_term.shape[1]
    shares = parts.shape[0]
    scores = []
    for core in range(2):
        picked = [parts[i] for i in range(shares) if i // 2 % 2 == core]
        while len(picked) > 1:
            picked = [one + two for one, two in zip(picked[::2], picked[1::2])]
        mean_square = picked[0][:, rows:] / (QUERY_HEAD_COUNT * HEAD_SIZE)
        scores.append(picked[0][:, :rows] / jnp.sqrt(mean_square + 1e-05))
    position = (where[1] * 2 + where[0]) * rows + lax.broadcasted_iota(jnp.int32, (1, rows), 1)
    rolls = lengths.shape[0]
    mean = reward[0]
    for index in range(1, rolls):
        mean = mean + reward[index]
    mean = mean / rolls
    begin = jnp.zeros((1, rows), jnp.int32)
    prompt = jnp.zeros((1, rows), jnp.int32) + prompt_len[0]
    advantage = jnp.zeros((1, rows), jnp.float32) + (reward[0] - mean)
    start = jnp.int32(0)
    for index in range(1, rolls):
        start = start + lengths[index - 1]
        inside = position >= start
        begin = jnp.where(inside, start, begin)
        prompt = jnp.where(inside, prompt_len[index], prompt)
        advantage = jnp.where(inside, reward[index] - mean, advantage)
    answer = jnp.where(position - begin >= prompt, 1.0, 0.0)
    gap = scores[1] - scores[0]
    term = answer * (jnp.exp(gap) - gap - 1.0)
    kl_term[...] = term
    objective[...] = answer * advantage - BETA * term


def products(held, weights, low, front, store):
    wide = GROUP * HEAD_SIZE
    query_w, key_w, value_w = weights
    for turn in range(2):
        first = pl.multiple_of((low + (front ^ turn)) * wide, HEAD_SIZE)
        total = jnp.dot(
            held, query_w[0, :, pl.ds(first, wide)], preferred_element_type=jnp.float32
        )
        store(turn, 0, total * LINK_SCALE)
    for index, weight in enumerate((key_w, value_w)):
        first = pl.multiple_of(low * HEAD_SIZE, HEAD_SIZE)
        total = jnp.dot(
            held, weight[0, :, pl.ds(first, 2 * HEAD_SIZE)], preferred_element_type=jnp.float32
        )
        total = total * LINK_SCALE
        lower, upper = total[:, :HEAD_SIZE], total[:, HEAD_SIZE:]
        for turn, (one, two) in enumerate(((lower, upper), (upper, lower))):
            store(turn, wide + index * HEAD_SIZE, jnp.where(front == 0, one, two))


def own_kernel(plan, own, other, query_w, key_w, value_w, out, sources):
    held = jnp.concatenate([own[...], other[...]], axis=0)
    for pair in range(2):

        def store(turn, start, total):
            out[2 * pair + turn, :, start : start + total.shape[1]] = total

        low, front = plan[sources + 2 * pair], plan[sources + 2 * pair + 1]
        products(held, (query_w, key_w, value_w), low, front, store)


def rest_kernel(plan, *refs, pair):
    pieces = refs[:-7]
    own, query_w, key_w, value_w, *outs, tokens = refs[-7:]
    rows = pieces[0].shape[0]
    chip = 2 * rows
    sources = len(pieces) // 2

    def place(slot):
        return pl.ds(pl.multiple_of(plan[slot] * chip, chip), chip)

    for index, piece in enumerate(pieces):
        tokens[index * rows : (index + 1) * rows, :] = piece[...]
    for turn in range(2):
        outs[turn][place(sources), :] = own[2 * pair + turn]

    def store(turn, start, total):
        for slot in range(sources):
            part = total[slot * chip : (slot + 1) * chip, :]
            outs[turn][place(slot), start : start + total.shape[1]] = part

    low, front = plan[sources + 1 + 2 * pair], plan[sources + 2 + 2 * pair]
    products(tokens[...], (query_w, key_w, value_w), low, front, store)


def partial_call(kernel, shapes, operands, scratch, tokens, owners):
    vmem = pl.BlockSpec(memory_space=pltpu.VMEM)
    smem = pl.BlockSpec(memory_space=pltpu.SMEM)
    depth = operands[1].shape[1]
    cols = (GROUP + 2) * HEAD_SIZE
    return pl.pallas_call(
        kernel,
        out_shape=[jax.ShapeDtypeStruct(shape, jnp.float32) for shape in shapes],
        in_specs=[vmem if operand.ndim > 1 else smem for operand in operands],
        out_specs=[vmem for _ in shapes],
        scratch_shapes=scratch,
        compiler_params=pltpu.CompilerParams(vmem_limit_bytes=GRANT * 1024 * 1024),
        cost_estimate=pl.CostEstimate(
            flops=int(PRICE * 2 * owners * tokens * depth * cols),
            bytes_accessed=int(PRICE * 2 * (tokens * depth + owners * cols * (depth + 2 * tokens))),
            transcendentals=0,
        ),
    )(*operands)


def split_shards(
    hidden, w_query, key_projection, value_projection, score_head, lengths, prompt_len, reward
):
    rows = hidden.shape[0]
    depth = w_query.shape[1]
    ctx = lax.axis_index("ctx")
    section = lax.axis_index("sec")
    count = 4
    f16, f32 = jnp.float16, jnp.float32

    def columns(target):
        return lax.dynamic_slice_in_dim(hidden, (target % count) * depth, depth, 1)

    steps = (2, 1, 3)
    pieces = []
    for step in steps:
        pairs = [(i, (i + step) % count) for i in range(count)]
        pieces.append(lax.ppermute(columns(ctx + step), "ctx", pairs))
    mine = columns(ctx)
    weights = (w_query, key_projection, value_projection)
    cols = (GROUP + 2) * HEAD_SIZE
    chip = 2 * rows
    left = ctx < 2
    low = jnp.where(left, 2, 0)
    plan = jnp.stack(
        [*((ctx - step) % count for step in steps), ctx]
        + [low, jnp.where(left, 1, 0), 2 - low, 1 - ctx % 2]
    ).astype(jnp.int32)
    (own,) = partial_call(
        lambda *refs: own_kernel(*refs, sources=count),
        [(count, chip, cols)],
        (plan, mine, swapped(mine, "sec", 0), *weights),
        [],
        chip,
        count,
    )

    *pieces, own = lax.optimization_barrier((*pieces, own))
    pieces = [part for piece in pieces for part in (piece, swapped(piece, "sec", 0))]

    def rest(pair):
        return partial_call(
            lambda *refs: rest_kernel(*refs, pair=pair),
            [(count * chip, cols)] * 2,
            (plan, *pieces, own, *weights),
            [pltpu.VMEM((len(pieces) * rows, depth), jnp.bfloat16)],
            len(pieces) * rows,
            2,
        )

    first = rest(0)
    second = rest(1)

    def reduced(first, second):
        far = first[0].astype(f16)
        fold = lax.ppermute(far, "ctx", [(0, 1), (3, 2)])
        inner = first[1].astype(f16)
        middle = lax.ppermute(inner, "ctx", [(1, 2), (2, 1)])
        skip = lax.ppermute(inner, "ctx", [(0, 2), (3, 1)])
        folded = (far.astype(f32) + fold.astype(f32)).astype(f16)
        ends = lax.ppermute(folded, "ctx", [(1, 3), (2, 0)])
        beside, _ = lax.optimization_barrier((second[0].astype(f16), folded))
        near = lax.ppermute(beside, "ctx", [(0, 1), (1, 0), (2, 3), (3, 2)])
        total = second[1].astype(f16).astype(f32)
        for part in (middle, skip, near, ends):
            total = total + part.astype(f32)
        return (total * (1.0 / LINK_SCALE)).astype(jnp.bfloat16)

    mine = reduced(first, second)
    wide = GROUP * HEAD_SIZE
    smem = pl.BlockSpec(memory_space=pltpu.SMEM)
    where = jnp.stack([section, ctx]).astype(jnp.int32)
    sums = pl.pallas_call(
        lambda plan, *refs: attention_kernel(*refs, rows),
        out_shape=jax.ShapeDtypeStruct((4 * count, 1, 2 * rows), f32),
        grid_spec=pltpu.PrefetchScalarGridSpec(
            num_scalar_prefetch=1,
            grid=(1,),
            in_specs=[
                smem,
                smem,
                pl.BlockSpec(mine.shape, lambda i, plan: (0, 0)),
                pl.BlockSpec((1, wide), lambda i, plan: (0, plan[1])),
            ],
            out_specs=pl.BlockSpec((4 * count, 1, 2 * rows), lambda i, plan: (0, 0, 0)),
        ),
        compiler_params=pltpu.CompilerParams(vmem_limit_bytes=12 * 1024 * 1024),
    )(where, lengths, where, mine, score_head)

    spread = lax.all_to_all(sums, ("ctx", "sec", "tp"), 0, 0, tiled=True)
    vmem = pl.BlockSpec(memory_space=pltpu.VMEM)
    kl_term, objective = pl.pallas_call(
        final_kernel,
        out_shape=[jax.ShapeDtypeStruct((1, rows), f32)] * 2,
        in_specs=[smem, smem, smem, smem, vmem],
        out_specs=[vmem, vmem],
    )(lengths, prompt_len, reward, where, spread)
    return (kl_term.reshape(rows), objective.reshape(rows))


def solution(mesh):
    placed = (
        P(("grp", "ctx", "sec"), None),
        P("sec", "ctx", "tp"),
        P("sec", "ctx", "tp"),
        P("sec", "ctx", "tp"),
        P("sec", "tp"),
        P("grp"),
        P("grp"),
        P("grp"),
    )
    own_heads = KEY_VALUE_HEADS // mesh.shape["tp"]
    by_heads = mesh.shape["ctx"] == 4 and own_heads == 4
    return jax.shard_map(
        split_shards if by_heads else gathered_shards,
        mesh=mesh,
        in_specs=placed,
        out_specs=(P(("grp", "ctx", "sec")), P(("grp", "ctx", "sec"))),
        check_vma=False,
    )
```

```python
import jax
import jax.numpy as jnp
from jax import lax
from jax.experimental import pallas as pl
from jax.experimental.pallas import tpu as pltpu
from jax.sharding import PartitionSpec as P

QUERY_HEAD_COUNT = 32
KEY_VALUE_HEADS = 8
HEAD_SIZE = 128


BETA = 0.1
NEGATIVE = -1e30
LINK_SCALE = 16.0
GROUP = QUERY_HEAD_COUNT // KEY_VALUE_HEADS
GRANT = 12


def swapped(array, axis, distance):
    return lax.ppermute(array, axis, [(i, i ^ 1 << distance) for i in range(lax.axis_size(axis))])


def rollout_tables(lengths, prompt_len, reward, position):
    starts = jnp.cumsum(lengths) - lengths
    inside = starts[None, :] <= position[:, None]
    begin = jnp.max(jnp.where(inside, starts[None, :], 0), axis=1)
    latest = jnp.sum(inside.astype(jnp.int32), axis=1) - 1
    chosen = jnp.arange(lengths.shape[0], dtype=jnp.int32)[None, :] == latest[:, None]
    prompt = jnp.sum(jnp.where(chosen, prompt_len[None, :], 0), axis=1)
    centred = reward - jnp.mean(reward)
    advantage = jnp.sum(
        jnp.where(chosen, centred[None, :], jnp.zeros_like(centred)[None, :]), axis=1
    )
    answer = (position - begin >= prompt).astype(reward.dtype)
    return (begin, answer, advantage)


def gathered_shards(
    hidden, w_query, key_projection, value_projection, score_head, lengths, prompt_len, reward
):
    row_block = lax.all_gather(hidden, "sec", axis=0, tiled=True)
    token_rows = row_block.shape[0]
    query_w = w_query[0]
    key_w = key_projection[0]
    value_w = value_projection[0]
    head_w = score_head[0]
    query_cols = query_w.shape[1]
    pair_cols = key_w.shape[1]

    def add_rows(piece):
        return jnp.dot(row_block, piece, preferred_element_type=jnp.float32)

    query_rows = add_rows(lax.all_gather(query_w, "ctx", axis=0, tiled=True))
    key_rows = add_rows(lax.all_gather(key_w, "ctx", axis=0, tiled=True))
    value_rows = add_rows(lax.all_gather(value_w, "ctx", axis=0, tiled=True))
    query_rows = query_rows.astype(jnp.bfloat16)
    key_rows = key_rows.astype(jnp.bfloat16)
    value_rows = value_rows.astype(jnp.bfloat16)
    heads_here = pair_cols // HEAD_SIZE
    score_scale = HEAD_SIZE ** (-0.5)
    row_pos = lax.axis_index("ctx") * token_rows + jnp.arange(token_rows, dtype=jnp.int32)
    begin, answer, advantage = rollout_tables(lengths, prompt_len, reward, row_pos)
    first_begin = jnp.min(begin)
    last_row = row_pos[token_rows - 1]
    query_heads = query_rows.reshape(token_rows, heads_here, GROUP, HEAD_SIZE)
    start_state = (
        jnp.full((heads_here, GROUP, token_rows), NEGATIVE, jnp.float32),
        jnp.zeros((heads_here, GROUP, token_rows), jnp.float32),
        jnp.zeros((heads_here, GROUP, token_rows, HEAD_SIZE), jnp.float32),
    )
    key_piece = lax.all_gather(key_rows, "ctx", axis=0, tiled=True)
    value_piece = lax.all_gather(value_rows, "ctx", axis=0, tiled=True)
    count = key_piece.shape[0] // token_rows

    def tile_step(index, carried):
        offset = index * token_rows
        key_tile = lax.dynamic_slice_in_dim(key_piece, offset, token_rows, 0).reshape(
            token_rows, heads_here, HEAD_SIZE
        )
        value_tile = lax.dynamic_slice_in_dim(value_piece, offset, token_rows, 0).reshape(
            token_rows, heads_here, HEAD_SIZE
        )
        key_pos = offset + jnp.arange(token_rows, dtype=jnp.int32)

        def update(current):
            peak, weight_sum, mixed_values = current
            score_logits = (
                jnp.einsum(
                    "rkgd,pkd->kgrp", query_heads, key_tile, preferred_element_type=jnp.float32
                )
                * score_scale
            )
            valid = (key_pos[None, :] <= row_pos[:, None]) & (key_pos[None, :] >= begin[:, None])
            masked = jnp.where(valid[None, None], score_logits, NEGATIVE)
            new_peak = jnp.maximum(peak, jnp.max(masked, axis=3))
            weights = jnp.where(
                valid[None, None],
                jnp.exp(score_logits - new_peak[..., None]),
                jnp.zeros_like(score_logits),
            )
            factor = jnp.exp(peak - new_peak)
            new_sum = weight_sum * factor + jnp.sum(weights, axis=3)
            product = jnp.einsum(
                "kgrp,pkd->kgrd",
                weights.astype(jnp.bfloat16),
                value_tile,
                preferred_element_type=jnp.float32,
            )
            return (new_peak, new_sum, mixed_values * factor[..., None] + product)

        live = (offset <= last_row) & (offset + token_rows - 1 >= first_begin)
        return lax.cond(live, update, lambda kept: kept, carried)

    peak, weight_sum, mixed_values = lax.fori_loop(0, count, tile_step, start_state)
    attended = (
        (mixed_values / weight_sum[..., None]).transpose(2, 0, 1, 3).reshape(token_rows, query_cols)
    )
    numerator = jnp.dot(attended, head_w.astype(jnp.float32), precision=lax.Precision.HIGHEST)
    squares = jnp.sum(attended * attended, axis=1)
    section = lax.axis_index("sec")
    total_num, total_sq = lax.psum((numerator, squares), "tp")
    score = total_num / jnp.sqrt(total_sq / (QUERY_HEAD_COUNT * HEAD_SIZE) + 1e-05)
    other = swapped(score, "sec", 0)
    policy = jnp.where(section == 0, score, other)
    frozen = jnp.where(section == 0, other, score)
    gap = frozen - policy
    kl_full = answer * (jnp.exp(gap) - gap - 1.0)
    objective_full = answer * advantage - BETA * kl_full
    half = token_rows // 2
    kl_term = lax.dynamic_slice_in_dim(kl_full, section * half, half, 0)
    objective = lax.dynamic_slice_in_dim(objective_full, section * half, half, 0)
    return (kl_term, objective)


def token_places(index, section, rows):
    chip = 2 * rows
    row = lax.rem(index, chip)
    return index - row + lax.rem(row + section * rows, chip)


def attention_kernel(lengths, where, block, head, out, rows):
    tokens = block.shape[0]
    section = where[0]

    def place(shape, axis):
        return token_places(lax.broadcasted_iota(jnp.int32, shape, axis), section, rows)

    query_pos = place((1, tokens), 1)
    begin = jnp.zeros((1, tokens), jnp.int32)
    start = jnp.int32(0)
    for index in range(lengths.shape[0] - 1):
        start = start + lengths[index]
        begin = jnp.where(query_pos >= start, start, begin)
    key_pos = place((tokens, 1), 0)
    valid = (key_pos <= query_pos) & (key_pos >= begin)
    wide = GROUP * HEAD_SIZE
    key = block[:, wide : wide + HEAD_SIZE]
    value = block[:, wide + HEAD_SIZE :]
    numerator = jnp.zeros((1, tokens), jnp.float32)
    squares = jnp.zeros((1, tokens), jnp.float32)
    for index in range(GROUP):
        cols = slice(index * HEAD_SIZE, (index + 1) * HEAD_SIZE)
        logits = lax.dot_general(
            key, block[:, cols], (((1,), (1,)), ((), ())), preferred_element_type=jnp.float32
        ) * (HEAD_SIZE ** (-0.5))
        masked = jnp.where(valid, logits, NEGATIVE)
        peak = jnp.max(masked, axis=0, keepdims=True)
        weights = jnp.exp(masked - peak)
        total = jnp.sum(weights, axis=0, keepdims=True)
        mixed = lax.dot_general(
            value,
            weights.astype(jnp.bfloat16),
            (((0,), (0,)), ((), ())),
            preferred_element_type=jnp.float32,
        )
        attended = mixed / total
        column = jnp.broadcast_to(head[:, cols].astype(jnp.float32), (HEAD_SIZE, HEAD_SIZE)).T
        numerator += jnp.sum(attended * column[:, :1], axis=0, keepdims=True)
        squares += jnp.sum(attended * attended, axis=0, keepdims=True)
    for ctx in range(tokens // (2 * rows)):
        own = slice(2 * ctx * rows, (2 * ctx + 1) * rows)
        other = slice((2 * ctx + 1) * rows, (2 * ctx + 2) * rows)
        same, cross = (
            jnp.concatenate([numerator[:, part], squares[:, part]], axis=1)
            for part in (own, other)
        )
        for core in range(2):
            row = jnp.where(section == core, same, cross)
            for share in range(2):
                out[ctx * 4 + core * 2 + share] = row


def final_kernel(lengths, prompt_len, reward, where, parts, kl_term, objective):
    rows = kl_term.shape[1]
    shares = parts.shape[0]
    scores = []
    for core in range(2):
        picked = [parts[i] for i in range(shares) if i // 2 % 2 == core]
        while len(picked) > 1:
            picked = [one + two for one, two in zip(picked[::2], picked[1::2])]
        mean_square = picked[0][:, rows:] / (QUERY_HEAD_COUNT * HEAD_SIZE)
        scores.append(picked[0][:, :rows] / jnp.sqrt(mean_square + 1e-05))
    position = (where[1] * 2 + where[0]) * rows + lax.broadcasted_iota(jnp.int32, (1, rows), 1)
    rolls = lengths.shape[0]
    mean = reward[0]
    for index in range(1, rolls):
        mean = mean + reward[index]
    mean = mean / rolls
    begin = jnp.zeros((1, rows), jnp.int32)
    prompt = jnp.zeros((1, rows), jnp.int32) + prompt_len[0]
    advantage = jnp.zeros((1, rows), jnp.float32) + (reward[0] - mean)
    start = jnp.int32(0)
    for index in range(1, rolls):
        start = start + lengths[index - 1]
        inside = position >= start
        begin = jnp.where(inside, start, begin)
        prompt = jnp.where(inside, prompt_len[index], prompt)
        advantage = jnp.where(inside, reward[index] - mean, advantage)
    answer = jnp.where(position - begin >= prompt, 1.0, 0.0)
    gap = scores[1] - scores[0]
    term = answer * (jnp.exp(gap) - gap - 1.0)
    kl_term[...] = term
    objective[...] = answer * advantage - BETA * term


def products(held, weights, low, front, store):
    wide = GROUP * HEAD_SIZE
    query_w, key_w, value_w = weights
    for turn in range(2):
        first = pl.multiple_of((low + (front ^ turn)) * wide, HEAD_SIZE)
        total = jnp.dot(
            held, query_w[0, :, pl.ds(first, wide)], preferred_element_type=jnp.float32
        )
        store(turn, 0, total * LINK_SCALE)
    for index, weight in enumerate((key_w, value_w)):
        first = pl.multiple_of(low * HEAD_SIZE, HEAD_SIZE)
        total = jnp.dot(
            held, weight[0, :, pl.ds(first, 2 * HEAD_SIZE)], preferred_element_type=jnp.float32
        )
        total = total * LINK_SCALE
        lower, upper = total[:, :HEAD_SIZE], total[:, HEAD_SIZE:]
        for turn, (one, two) in enumerate(((lower, upper), (upper, lower))):
            store(turn, wide + index * HEAD_SIZE, jnp.where(front == 0, one, two))


def own_kernel(plan, own, other, query_w, key_w, value_w, out, sources):
    held = jnp.concatenate([own[...], other[...]], axis=0)
    for pair in range(2):

        def store(turn, start, total):
            out[2 * pair + turn, :, start : start + total.shape[1]] = total

        low, front = plan[sources + 2 * pair], plan[sources + 2 * pair + 1]
        products(held, (query_w, key_w, value_w), low, front, store)


def rest_kernel(plan, *refs, pair, layout):
    pieces = refs[: len(layout)]
    own, query_w, key_w, value_w, outs, tokens = refs[len(layout) :]
    chip = own.shape[1]
    sources = tokens.shape[0] // chip

    def place(slot):
        return pl.ds(pl.multiple_of(plan[slot] * chip, chip), chip)

    for piece, (base, half) in zip(pieces, layout):
        rows = piece.shape[0]
        if half is not None:
            base = pl.multiple_of(base + (plan[sources + 5] ^ half) * rows, rows)
        tokens[pl.ds(base, rows), :] = piece[...]
    for turn in range(2):
        outs[turn, place(sources), :] = own[2 * pair + turn]

    def store(turn, start, total):
        for slot in range(sources):
            part = total[slot * chip : (slot + 1) * chip, :]
            outs[turn, place(slot), start : start + total.shape[1]] = part

    low, front = plan[sources + 1 + 2 * pair], plan[sources + 2 + 2 * pair]
    products(tokens[...], (query_w, key_w, value_w), low, front, store)


def partial_call(kernel, shapes, operands, scratch, tokens, owners):
    vmem = pl.BlockSpec(memory_space=pltpu.VMEM)
    smem = pl.BlockSpec(memory_space=pltpu.SMEM)
    depth = operands[1].shape[1]
    cols = (GROUP + 2) * HEAD_SIZE
    return pl.pallas_call(
        kernel,
        out_shape=[jax.ShapeDtypeStruct(shape, jnp.float32) for shape in shapes],
        in_specs=[vmem if operand.ndim > 1 else smem for operand in operands],
        out_specs=[vmem for _ in shapes],
        scratch_shapes=scratch,
        compiler_params=pltpu.CompilerParams(vmem_limit_bytes=GRANT * 1024 * 1024),
        cost_estimate=pl.CostEstimate(
            flops=int(2 * owners * tokens * depth * cols),
            bytes_accessed=int(2 * (tokens * depth + owners * cols * (depth + 2 * tokens))),
            transcendentals=0,
        ),
    )(*operands)


def split_shards(
    hidden, w_query, key_projection, value_projection, score_head, lengths, prompt_len, reward
):
    rows = hidden.shape[0]
    depth = w_query.shape[1]
    ctx = lax.axis_index("ctx")
    section = lax.axis_index("sec")
    share = lax.axis_index("tp")
    count = 4
    f16, f32 = jnp.float16, jnp.float32

    steps = (2, 1, 3)
    half_rows = rows // 2
    sent = {}
    for step in steps:
        pairs = [(i, (i + step) % count) for i in range(count)]
        start = ((ctx + step) % count) * depth
        if step == 2:
            piece = lax.dynamic_slice(hidden, (share * half_rows, start), (half_rows, depth))
        else:
            piece = lax.dynamic_slice_in_dim(hidden, start, depth, 1)
        sent[step] = lax.ppermute(piece, "ctx", pairs)
    mine = lax.dynamic_slice_in_dim(hidden, ctx * depth, depth, 1)
    weights = (w_query, key_projection, value_projection)
    cols = (GROUP + 2) * HEAD_SIZE
    chip = 2 * rows
    left = ctx < 2
    low = jnp.where(left, 2, 0)
    plan = jnp.stack(
        [*((ctx - step) % count for step in steps), ctx]
        + [low, jnp.where(left, 1, 0), 2 - low, 1 - ctx % 2, share]
    ).astype(jnp.int32)
    (own,) = partial_call(
        lambda *refs: own_kernel(*refs, sources=count),
        [(count, chip, cols)],
        (plan, mine, swapped(mine, "sec", 0), *weights),
        [],
        chip,
        count,
    )

    sent[2], own = lax.optimization_barrier((sent[2], own))
    swap = swapped(sent[2], "tp", 0)
    sent[1], sent[3], swap, own = lax.optimization_barrier((sent[1], sent[3], swap, own))
    pieces, layout = [], []
    for slot, step in enumerate(steps):
        parts = [(sent[step], None)]
        if step == 2:
            parts = [(sent[step], 0), (swap, 1)]
        for part, half in parts:
            pieces += [part, swapped(part, "sec", 0)]
            layout += [(slot * chip, half), (slot * chip + rows, half)]

    def rest(pair):
        return partial_call(
            lambda *refs: rest_kernel(*refs, pair=pair, layout=layout),
            [(2, count * chip, cols)],
            (plan, *pieces, own, *weights),
            [pltpu.VMEM((len(steps) * chip, depth), jnp.bfloat16)],
            len(steps) * chip,
            2,
        )[0]

    first = rest(0)
    second = rest(1)

    def reduced(first, second):
        fold = lax.ppermute(first[0].astype(f16), "ctx", [(0, 1), (3, 2)])
        inner = first[1].astype(f16)
        middle = lax.ppermute(inner, "ctx", [(1, 2), (2, 1)])
        skip = lax.ppermute(inner, "ctx", [(0, 2), (3, 1)])
        folded = (first[0] + fold.astype(f32)).astype(f16)
        ends = lax.ppermute(folded, "ctx", [(1, 3), (2, 0)])
        beside, _ = lax.optimization_barrier((second[0].astype(f16), folded))
        near = lax.ppermute(beside, "ctx", [(0, 1), (1, 0), (2, 3), (3, 2)])
        total = second[1]
        for part in (middle, skip, near, ends):
            total = total + part.astype(f32)
        return (total * (1.0 / LINK_SCALE)).astype(jnp.bfloat16)

    mine = reduced(first, second)
    wide = GROUP * HEAD_SIZE
    smem = pl.BlockSpec(memory_space=pltpu.SMEM)
    where = jnp.stack([section, ctx]).astype(jnp.int32)
    sums = pl.pallas_call(
        lambda plan, *refs: attention_kernel(*refs, rows),
        out_shape=jax.ShapeDtypeStruct((4 * count, 1, 2 * rows), f32),
        grid_spec=pltpu.PrefetchScalarGridSpec(
            num_scalar_prefetch=1,
            grid=(1,),
            in_specs=[
                smem,
                smem,
                pl.BlockSpec(mine.shape, lambda i, plan: (0, 0)),
                pl.BlockSpec((1, wide), lambda i, plan: (0, plan[1])),
            ],
            out_specs=pl.BlockSpec((4 * count, 1, 2 * rows), lambda i, plan: (0, 0, 0)),
        ),
        compiler_params=pltpu.CompilerParams(vmem_limit_bytes=12 * 1024 * 1024),
    )(where, lengths, where, mine, score_head)

    spread = lax.all_to_all(sums, ("ctx", "sec", "tp"), 0, 0, tiled=True)
    vmem = pl.BlockSpec(memory_space=pltpu.VMEM)
    kl_term, objective = pl.pallas_call(
        final_kernel,
        out_shape=[jax.ShapeDtypeStruct((1, rows), f32)] * 2,
        in_specs=[smem, smem, smem, smem, vmem],
        out_specs=[vmem, vmem],
    )(lengths, prompt_len, reward, where, spread)
    return (kl_term.reshape(rows), objective.reshape(rows))


def solution(mesh):
    placed = (
        P(("grp", "ctx", "sec"), None),
        P("sec", "ctx", "tp"),
        P("sec", "ctx", "tp"),
        P("sec", "ctx", "tp"),
        P("sec", "tp"),
        P("grp"),
        P("grp"),
        P("grp"),
    )
    own_heads = KEY_VALUE_HEADS // mesh.shape["tp"]
    by_heads = mesh.shape["ctx"] == 4 and own_heads == 4
    return jax.shard_map(
        split_shards if by_heads else gathered_shards,
        mesh=mesh,
        in_specs=placed,
        out_specs=(P(("grp", "ctx", "sec")), P(("grp", "ctx", "sec"))),
        check_vma=False,
    )
```

```python
import math

import jax
import jax.numpy as jnp
from jax import lax
from jax.experimental import pallas as pl
from jax.experimental.pallas import tpu as pltpu
from jax.sharding import PartitionSpec as P

QUERY_HEAD_COUNT = 32
KEY_VALUE_HEADS = 8
HEAD_SIZE = 128


BETA = 0.1
NEGATIVE = -1e30
LINK_SCALE = 16.0
GROUP = QUERY_HEAD_COUNT // KEY_VALUE_HEADS
GRANT = 12


def swapped(array, axis, distance):
    return lax.ppermute(array, axis, [(i, i ^ 1 << distance) for i in range(lax.axis_size(axis))])


def rollout_tables(lengths, prompt_len, reward, position):
    starts = jnp.cumsum(lengths) - lengths
    inside = starts[None, :] <= position[:, None]
    begin = jnp.max(jnp.where(inside, starts[None, :], 0), axis=1)
    latest = jnp.sum(inside.astype(jnp.int32), axis=1) - 1
    chosen = jnp.arange(lengths.shape[0], dtype=jnp.int32)[None, :] == latest[:, None]
    prompt = jnp.sum(jnp.where(chosen, prompt_len[None, :], 0), axis=1)
    centred = reward - jnp.mean(reward)
    advantage = jnp.sum(
        jnp.where(chosen, centred[None, :], jnp.zeros_like(centred)[None, :]), axis=1
    )
    answer = (position - begin >= prompt).astype(reward.dtype)
    return (begin, answer, advantage)


def gathered_shards(
    hidden, w_query, key_projection, value_projection, score_head, lengths, prompt_len, reward
):
    row_block = lax.all_gather(hidden, "sec", axis=0, tiled=True)
    token_rows = row_block.shape[0]
    query_w = w_query[0]
    key_w = key_projection[0]
    value_w = value_projection[0]
    head_w = score_head[0]
    query_cols = query_w.shape[1]
    pair_cols = key_w.shape[1]

    def add_rows(piece):
        return jnp.dot(row_block, piece, preferred_element_type=jnp.float32)

    query_rows = add_rows(lax.all_gather(query_w, "ctx", axis=0, tiled=True))
    key_rows = add_rows(lax.all_gather(key_w, "ctx", axis=0, tiled=True))
    value_rows = add_rows(lax.all_gather(value_w, "ctx", axis=0, tiled=True))
    query_rows = query_rows.astype(jnp.bfloat16)
    key_rows = key_rows.astype(jnp.bfloat16)
    value_rows = value_rows.astype(jnp.bfloat16)
    heads_here = pair_cols // HEAD_SIZE
    score_scale = HEAD_SIZE ** (-0.5)
    row_pos = lax.axis_index("ctx") * token_rows + jnp.arange(token_rows, dtype=jnp.int32)
    begin, answer, advantage = rollout_tables(lengths, prompt_len, reward, row_pos)
    first_begin = jnp.min(begin)
    last_row = row_pos[token_rows - 1]
    query_heads = query_rows.reshape(token_rows, heads_here, GROUP, HEAD_SIZE)
    start_state = (
        jnp.full((heads_here, GROUP, token_rows), NEGATIVE, jnp.float32),
        jnp.zeros((heads_here, GROUP, token_rows), jnp.float32),
        jnp.zeros((heads_here, GROUP, token_rows, HEAD_SIZE), jnp.float32),
    )
    key_piece = lax.all_gather(key_rows, "ctx", axis=0, tiled=True)
    value_piece = lax.all_gather(value_rows, "ctx", axis=0, tiled=True)
    count = key_piece.shape[0] // token_rows

    def tile_step(index, carried):
        offset = index * token_rows
        key_tile = lax.dynamic_slice_in_dim(key_piece, offset, token_rows, 0).reshape(
            token_rows, heads_here, HEAD_SIZE
        )
        value_tile = lax.dynamic_slice_in_dim(value_piece, offset, token_rows, 0).reshape(
            token_rows, heads_here, HEAD_SIZE
        )
        key_pos = offset + jnp.arange(token_rows, dtype=jnp.int32)

        def update(current):
            peak, weight_sum, mixed_values = current
            score_logits = (
                jnp.einsum(
                    "rkgd,pkd->kgrp", query_heads, key_tile, preferred_element_type=jnp.float32
                )
                * score_scale
            )
            valid = (key_pos[None, :] <= row_pos[:, None]) & (key_pos[None, :] >= begin[:, None])
            masked = jnp.where(valid[None, None], score_logits, NEGATIVE)
            new_peak = jnp.maximum(peak, jnp.max(masked, axis=3))
            weights = jnp.where(
                valid[None, None],
                jnp.exp(score_logits - new_peak[..., None]),
                jnp.zeros_like(score_logits),
            )
            factor = jnp.exp(peak - new_peak)
            new_sum = weight_sum * factor + jnp.sum(weights, axis=3)
            product = jnp.einsum(
                "kgrp,pkd->kgrd",
                weights.astype(jnp.bfloat16),
                value_tile,
                preferred_element_type=jnp.float32,
            )
            return (new_peak, new_sum, mixed_values * factor[..., None] + product)

        live = (offset <= last_row) & (offset + token_rows - 1 >= first_begin)
        return lax.cond(live, update, lambda kept: kept, carried)

    peak, weight_sum, mixed_values = lax.fori_loop(0, count, tile_step, start_state)
    attended = (
        (mixed_values / weight_sum[..., None]).transpose(2, 0, 1, 3).reshape(token_rows, query_cols)
    )
    numerator = jnp.dot(attended, head_w.astype(jnp.float32), precision=lax.Precision.HIGHEST)
    squares = jnp.sum(attended * attended, axis=1)
    section = lax.axis_index("sec")
    total_num, total_sq = lax.psum((numerator, squares), "tp")
    score = total_num / jnp.sqrt(total_sq / (QUERY_HEAD_COUNT * HEAD_SIZE) + 1e-05)
    other = swapped(score, "sec", 0)
    policy = jnp.where(section == 0, score, other)
    frozen = jnp.where(section == 0, other, score)
    gap = frozen - policy
    kl_full = answer * (jnp.exp(gap) - gap - 1.0)
    objective_full = answer * advantage - BETA * kl_full
    half = token_rows // 2
    kl_term = lax.dynamic_slice_in_dim(kl_full, section * half, half, 0)
    objective = lax.dynamic_slice_in_dim(objective_full, section * half, half, 0)
    return (kl_term, objective)


def token_places(index, section, rows):
    chip = 2 * rows
    row = lax.rem(index, chip)
    return index - row + lax.rem(row + section * rows, chip)


def attention_kernel(lengths, where, block, head, out, rows):
    tokens = block.shape[0]
    section = where[0]

    def place(shape, axis):
        return token_places(lax.broadcasted_iota(jnp.int32, shape, axis), section, rows)

    wide = GROUP * HEAD_SIZE
    columns = [
        jnp.broadcast_to(head[:, cols].astype(jnp.float32), (HEAD_SIZE, HEAD_SIZE)).T[:, :1]
        for cols in (slice(at, at + HEAD_SIZE) for at in range(0, wide, HEAD_SIZE))
    ]
    query_pos = place((1, tokens), 1)
    key_pos = place((tokens, 1), 0)
    begin = jnp.zeros((1, tokens), jnp.int32)
    start = jnp.int32(0)
    for index in range(lengths.shape[0] - 1):
        start = start + lengths[index]
        begin = jnp.where(query_pos >= start, start, begin)
    valid = (key_pos <= query_pos) & (key_pos >= begin)
    key = block[:, wide : wide + HEAD_SIZE]
    value = block[:, wide + HEAD_SIZE :]
    numerator = jnp.zeros((1, tokens), jnp.float32)
    squares = jnp.zeros((1, tokens), jnp.float32)
    for index in range(GROUP):
        logits = lax.dot_general(
            key,
            block[:, index * HEAD_SIZE : (index + 1) * HEAD_SIZE],
            (((1,), (1,)), ((), ())),
            preferred_element_type=jnp.float32,
        )
        masked = jnp.where(valid, logits, NEGATIVE)
        peak = jnp.max(masked, axis=0, keepdims=True)
        weights = jnp.exp2((masked - peak) * (HEAD_SIZE ** (-0.5) * math.log2(math.e)))
        total = jnp.sum(weights, axis=0, keepdims=True)
        mixed = lax.dot_general(
            value,
            weights.astype(jnp.bfloat16),
            (((0,), (0,)), ((), ())),
            preferred_element_type=jnp.float32,
        )
        attended = mixed * (1.0 / total)
        numerator += jnp.sum(attended * columns[index], axis=0, keepdims=True)
        squares += jnp.sum(attended * attended, axis=0, keepdims=True)
    for ctx in range(tokens // (2 * rows)):
        own = slice(2 * ctx * rows, (2 * ctx + 1) * rows)
        other = slice((2 * ctx + 1) * rows, (2 * ctx + 2) * rows)
        same, cross = (
            jnp.concatenate([numerator[:, part], squares[:, part]], axis=1)
            for part in (own, other)
        )
        for core in range(2):
            row = jnp.where(section == core, same, cross)
            for share in range(2):
                out[ctx * 4 + core * 2 + share] = row


def final_kernel(lengths, prompt_len, reward, where, parts, kl_term, objective):
    rows = kl_term.shape[1]
    shares = parts.shape[0]
    scores = []
    for core in range(2):
        picked = [parts[i] for i in range(shares) if i // 2 % 2 == core]
        while len(picked) > 1:
            picked = [one + two for one, two in zip(picked[::2], picked[1::2])]
        mean_square = picked[0][:, rows:] / (QUERY_HEAD_COUNT * HEAD_SIZE)
        scores.append(picked[0][:, :rows] / jnp.sqrt(mean_square + 1e-05))
    position = (where[1] * 2 + where[0]) * rows + lax.broadcasted_iota(jnp.int32, (1, rows), 1)
    rolls = lengths.shape[0]
    mean = reward[0]
    for index in range(1, rolls):
        mean = mean + reward[index]
    mean = mean / rolls
    begin = jnp.zeros((1, rows), jnp.int32)
    prompt = jnp.zeros((1, rows), jnp.int32) + prompt_len[0]
    advantage = jnp.zeros((1, rows), jnp.float32) + (reward[0] - mean)
    start = jnp.int32(0)
    for index in range(1, rolls):
        start = start + lengths[index - 1]
        inside = position >= start
        begin = jnp.where(inside, start, begin)
        prompt = jnp.where(inside, prompt_len[index], prompt)
        advantage = jnp.where(inside, reward[index] - mean, advantage)
    answer = jnp.where(position - begin >= prompt, 1.0, 0.0)
    gap = scores[1] - scores[0]
    term = answer * (jnp.exp(gap) - gap - 1.0)
    kl_term[...] = term
    objective[...] = answer * advantage - BETA * term


def products(held, weights, low, front, store):
    wide = GROUP * HEAD_SIZE
    query_w, key_w, value_w = weights
    for turn in range(2):
        first = pl.multiple_of((low + (front ^ turn)) * wide, HEAD_SIZE)
        total = jnp.dot(
            held, query_w[0, :, pl.ds(first, wide)], preferred_element_type=jnp.float32
        )
        store(turn, 0, total * LINK_SCALE)
    for index, weight in enumerate((key_w, value_w)):
        first = pl.multiple_of(low * HEAD_SIZE, HEAD_SIZE)
        total = jnp.dot(
            held, weight[0, :, pl.ds(first, 2 * HEAD_SIZE)], preferred_element_type=jnp.float32
        )
        total = total * LINK_SCALE
        lower, upper = total[:, :HEAD_SIZE], total[:, HEAD_SIZE:]
        for turn, (one, two) in enumerate(((lower, upper), (upper, lower))):
            store(turn, wide + index * HEAD_SIZE, jnp.where(front == 0, one, two))


def cut_kernel(plan, hidden, *refs):
    outs, done = refs[:-1], refs[-1]
    copies = []
    for index, out in enumerate(outs):
        rows, depth = out.shape
        first = 0
        if rows < hidden.shape[0]:
            first = pl.multiple_of(plan[0] * rows, rows)
        start = pl.multiple_of(plan[1 + index] * depth, HEAD_SIZE)
        part = hidden.at[pl.ds(first, rows), pl.ds(start, depth)]
        copies.append(pltpu.make_async_copy(part, out, done.at[index]))
    for copy in copies:
        copy.start()
    for copy in copies:
        copy.wait()


def own_kernel(plan, own, other, query_w, key_w, value_w, out, sources):
    held = jnp.concatenate([own[...], other[...]], axis=0)
    for pair in range(2):

        def store(turn, start, total):
            out[2 * pair + turn, :, start : start + total.shape[1]] = total

        low, front = plan[sources + 2 * pair], plan[sources + 2 * pair + 1]
        products(held, (query_w, key_w, value_w), low, front, store)


def rest_kernel(plan, *refs, pair, layout):
    pieces = refs[: len(layout)]
    own, query_w, key_w, value_w, outs, tokens = refs[len(layout) :]
    chip = own.shape[1]
    sources = tokens.shape[0] // chip

    def place(slot):
        return pl.ds(pl.multiple_of(plan[slot] * chip, chip), chip)

    for piece, (base, half) in zip(pieces, layout):
        rows = piece.shape[0]
        if half is not None:
            base = pl.multiple_of(base + (plan[sources + 5] ^ half) * rows, rows)
        tokens[pl.ds(base, rows), :] = piece[...]
    for turn in range(2):
        outs[turn, place(sources), :] = own[2 * pair + turn]

    def store(turn, start, total):
        for slot in range(sources):
            part = total[slot * chip : (slot + 1) * chip, :]
            outs[turn, place(slot), start : start + total.shape[1]] = part

    low, front = plan[sources + 1 + 2 * pair], plan[sources + 2 + 2 * pair]
    products(tokens[...], (query_w, key_w, value_w), low, front, store)


def partial_call(kernel, shapes, operands, scratch, tokens, owners):
    vmem = pl.BlockSpec(memory_space=pltpu.VMEM)
    smem = pl.BlockSpec(memory_space=pltpu.SMEM)
    depth = operands[1].shape[1]
    cols = (GROUP + 2) * HEAD_SIZE
    return pl.pallas_call(
        kernel,
        out_shape=[jax.ShapeDtypeStruct(shape, jnp.float32) for shape in shapes],
        in_specs=[vmem if operand.ndim > 1 else smem for operand in operands],
        out_specs=[vmem for _ in shapes],
        scratch_shapes=scratch,
        compiler_params=pltpu.CompilerParams(vmem_limit_bytes=GRANT * 1024 * 1024),
        cost_estimate=pl.CostEstimate(
            flops=int(2 * owners * tokens * depth * cols),
            bytes_accessed=int(2 * (tokens * depth + owners * cols * (depth + 2 * tokens))),
            transcendentals=0,
        ),
    )(*operands)


def split_shards(
    hidden, w_query, key_projection, value_projection, score_head, lengths, prompt_len, reward
):
    rows = hidden.shape[0]
    depth = w_query.shape[1]
    ctx = lax.axis_index("ctx")
    section = lax.axis_index("sec")
    share = lax.axis_index("tp")
    count = 4
    f16, f32 = jnp.float16, jnp.float32

    steps = (2, 1, 3)
    half_rows = rows // 2
    targets = [(ctx + step) % count for step in (*steps, 0)]
    cuts = pl.pallas_call(
        cut_kernel,
        out_shape=[
            jax.ShapeDtypeStruct((half_rows if step == 2 else rows, depth), hidden.dtype)
            for step in (*steps, 0)
        ],
        in_specs=[
            pl.BlockSpec(memory_space=pltpu.SMEM),
            pl.BlockSpec(memory_space=pl.ANY),
        ],
        out_specs=[pl.BlockSpec(memory_space=pltpu.VMEM)] * 4,
        scratch_shapes=[pltpu.SemaphoreType.DMA((4,))],
        compiler_params=pltpu.CompilerParams(vmem_limit_bytes=4 * 1024 * 1024),
    )(jnp.stack([share, *targets]).astype(jnp.int32), hidden)
    mine = cuts[3]
    sent = {}
    for step, piece in zip(steps, cuts):
        pairs = [(i, (i + step) % count) for i in range(count)]
        sent[step] = lax.ppermute(piece, "ctx", pairs)
    weights = (w_query, key_projection, value_projection)
    cols = (GROUP + 2) * HEAD_SIZE
    chip = 2 * rows
    left = ctx < 2
    low = jnp.where(left, 2, 0)
    plan = jnp.stack(
        [*((ctx - step) % count for step in steps), ctx]
        + [low, jnp.where(left, 1, 0), 2 - low, 1 - ctx % 2, share]
    ).astype(jnp.int32)
    (own,) = partial_call(
        lambda *refs: own_kernel(*refs, sources=count),
        [(count, chip, cols)],
        (plan, mine, swapped(mine, "sec", 0), *weights),
        [],
        chip,
        count,
    )

    sent[2], own = lax.optimization_barrier((sent[2], own))
    swap = swapped(sent[2], "tp", 0)
    sent[1], sent[3], swap, own = lax.optimization_barrier((sent[1], sent[3], swap, own))
    pieces, layout = [], []
    for slot, step in enumerate(steps):
        parts = [(sent[step], None)]
        if step == 2:
            parts = [(sent[step], 0), (swap, 1)]
        for part, half in parts:
            pieces += [part, swapped(part, "sec", 0)]
            layout += [(slot * chip, half), (slot * chip + rows, half)]

    def rest(pair):
        return partial_call(
            lambda *refs: rest_kernel(*refs, pair=pair, layout=layout),
            [(2, count * chip, cols)],
            (plan, *pieces, own, *weights),
            [pltpu.VMEM((len(steps) * chip, depth), jnp.bfloat16)],
            len(steps) * chip,
            2,
        )[0]

    first = rest(0)
    second = rest(1)

    def reduced(first, second):
        far, first = lax.optimization_barrier((first[0].astype(f16), first))
        fold = lax.ppermute(far, "ctx", [(0, 1), (3, 2)])
        inner = first[1].astype(f16)
        middle = lax.ppermute(inner, "ctx", [(1, 2), (2, 1)])
        skip = lax.ppermute(inner, "ctx", [(0, 2), (3, 1)])
        folded = (first[0] + fold.astype(f32)).astype(f16)
        ends = lax.ppermute(folded, "ctx", [(1, 3), (2, 0)])
        beside, _ = lax.optimization_barrier((second[0].astype(f16), folded))
        near = lax.ppermute(beside, "ctx", [(0, 1), (1, 0), (2, 3), (3, 2)])
        total = second[1] + middle.astype(f32) + skip.astype(f32)
        total, near, ends = lax.optimization_barrier((total, near, ends))
        total = total + near.astype(f32) + ends.astype(f32)
        return (total * (1.0 / LINK_SCALE)).astype(jnp.bfloat16)

    mine = reduced(first, second)
    wide = GROUP * HEAD_SIZE
    smem = pl.BlockSpec(memory_space=pltpu.SMEM)
    where = jnp.stack([section, ctx]).astype(jnp.int32)
    sums = pl.pallas_call(
        lambda plan, *refs: attention_kernel(*refs, rows),
        out_shape=jax.ShapeDtypeStruct((4 * count, 1, 2 * rows), f32),
        grid_spec=pltpu.PrefetchScalarGridSpec(
            num_scalar_prefetch=1,
            grid=(1,),
            in_specs=[
                smem,
                smem,
                pl.BlockSpec(mine.shape, lambda i, plan: (0, 0)),
                pl.BlockSpec((1, wide), lambda i, plan: (0, plan[1])),
            ],
            out_specs=pl.BlockSpec((4 * count, 1, 2 * rows), lambda i, plan: (0, 0, 0)),
        ),
        compiler_params=pltpu.CompilerParams(vmem_limit_bytes=12 * 1024 * 1024),
    )(where, lengths, where, mine, score_head)

    spread = lax.all_to_all(sums, ("ctx", "sec", "tp"), 0, 0, tiled=True)
    vmem = pl.BlockSpec(memory_space=pltpu.VMEM)
    kl_term, objective = pl.pallas_call(
        final_kernel,
        out_shape=[jax.ShapeDtypeStruct((1, rows), f32)] * 2,
        in_specs=[smem, smem, smem, smem, vmem],
        out_specs=[vmem, vmem],
        compiler_params=pltpu.CompilerParams(vmem_limit_bytes=4 * 1024 * 1024),
    )(lengths, prompt_len, reward, where, spread)
    return (kl_term.reshape(rows), objective.reshape(rows))


def solution(mesh):
    placed = (
        P(("grp", "ctx", "sec"), None),
        P("sec", "ctx", "tp"),
        P("sec", "ctx", "tp"),
        P("sec", "ctx", "tp"),
        P("sec", "tp"),
        P("grp"),
        P("grp"),
        P("grp"),
    )
    own_heads = KEY_VALUE_HEADS // mesh.shape["tp"]
    by_heads = mesh.shape["ctx"] == 4 and own_heads == 4
    return jax.shard_map(
        split_shards if by_heads else gathered_shards,
        mesh=mesh,
        in_specs=placed,
        out_specs=(P(("grp", "ctx", "sec")), P(("grp", "ctx", "sec"))),
        check_vma=False,
    )
```

```python
import math

import jax
import jax.numpy as jnp
from jax import lax
from jax.experimental import pallas as pl
from jax.experimental.pallas import tpu as pltpu
from jax.sharding import PartitionSpec as P

QUERY_HEAD_COUNT = 32
KEY_VALUE_HEADS = 8
HEAD_SIZE = 128


BETA = 0.1
NEGATIVE = -1e30
LINK_SCALE = 16.0
GROUP = QUERY_HEAD_COUNT // KEY_VALUE_HEADS
GRANT = 12


def swapped(array, axis, distance):
    return lax.ppermute(array, axis, [(i, i ^ 1 << distance) for i in range(lax.axis_size(axis))])


def rollout_tables(lengths, prompt_len, reward, position):
    starts = jnp.cumsum(lengths) - lengths
    inside = starts[None, :] <= position[:, None]
    begin = jnp.max(jnp.where(inside, starts[None, :], 0), axis=1)
    latest = jnp.sum(inside.astype(jnp.int32), axis=1) - 1
    chosen = jnp.arange(lengths.shape[0], dtype=jnp.int32)[None, :] == latest[:, None]
    prompt = jnp.sum(jnp.where(chosen, prompt_len[None, :], 0), axis=1)
    centred = reward - jnp.mean(reward)
    advantage = jnp.sum(
        jnp.where(chosen, centred[None, :], jnp.zeros_like(centred)[None, :]), axis=1
    )
    answer = (position - begin >= prompt).astype(reward.dtype)
    return (begin, answer, advantage)


def gathered_shards(
    hidden, w_query, key_projection, value_projection, score_head, lengths, prompt_len, reward
):
    row_block = lax.all_gather(hidden, "sec", axis=0, tiled=True)
    token_rows = row_block.shape[0]
    query_w = w_query[0]
    key_w = key_projection[0]
    value_w = value_projection[0]
    head_w = score_head[0]
    query_cols = query_w.shape[1]
    pair_cols = key_w.shape[1]

    def add_rows(piece):
        return jnp.dot(row_block, piece, preferred_element_type=jnp.float32)

    query_rows = add_rows(lax.all_gather(query_w, "ctx", axis=0, tiled=True))
    key_rows = add_rows(lax.all_gather(key_w, "ctx", axis=0, tiled=True))
    value_rows = add_rows(lax.all_gather(value_w, "ctx", axis=0, tiled=True))
    query_rows = query_rows.astype(jnp.bfloat16)
    key_rows = key_rows.astype(jnp.bfloat16)
    value_rows = value_rows.astype(jnp.bfloat16)
    heads_here = pair_cols // HEAD_SIZE
    score_scale = HEAD_SIZE ** (-0.5)
    row_pos = lax.axis_index("ctx") * token_rows + jnp.arange(token_rows, dtype=jnp.int32)
    begin, answer, advantage = rollout_tables(lengths, prompt_len, reward, row_pos)
    first_begin = jnp.min(begin)
    last_row = row_pos[token_rows - 1]
    query_heads = query_rows.reshape(token_rows, heads_here, GROUP, HEAD_SIZE)
    start_state = (
        jnp.full((heads_here, GROUP, token_rows), NEGATIVE, jnp.float32),
        jnp.zeros((heads_here, GROUP, token_rows), jnp.float32),
        jnp.zeros((heads_here, GROUP, token_rows, HEAD_SIZE), jnp.float32),
    )
    key_piece = lax.all_gather(key_rows, "ctx", axis=0, tiled=True)
    value_piece = lax.all_gather(value_rows, "ctx", axis=0, tiled=True)
    count = key_piece.shape[0] // token_rows

    def tile_step(index, carried):
        offset = index * token_rows
        key_tile = lax.dynamic_slice_in_dim(key_piece, offset, token_rows, 0).reshape(
            token_rows, heads_here, HEAD_SIZE
        )
        value_tile = lax.dynamic_slice_in_dim(value_piece, offset, token_rows, 0).reshape(
            token_rows, heads_here, HEAD_SIZE
        )
        key_pos = offset + jnp.arange(token_rows, dtype=jnp.int32)

        def update(current):
            peak, weight_sum, mixed_values = current
            score_logits = (
                jnp.einsum(
                    "rkgd,pkd->kgrp", query_heads, key_tile, preferred_element_type=jnp.float32
                )
                * score_scale
            )
            valid = (key_pos[None, :] <= row_pos[:, None]) & (key_pos[None, :] >= begin[:, None])
            masked = jnp.where(valid[None, None], score_logits, NEGATIVE)
            new_peak = jnp.maximum(peak, jnp.max(masked, axis=3))
            weights = jnp.where(
                valid[None, None],
                jnp.exp(score_logits - new_peak[..., None]),
                jnp.zeros_like(score_logits),
            )
            factor = jnp.exp(peak - new_peak)
            new_sum = weight_sum * factor + jnp.sum(weights, axis=3)
            product = jnp.einsum(
                "kgrp,pkd->kgrd",
                weights.astype(jnp.bfloat16),
                value_tile,
                preferred_element_type=jnp.float32,
            )
            return (new_peak, new_sum, mixed_values * factor[..., None] + product)

        live = (offset <= last_row) & (offset + token_rows - 1 >= first_begin)
        return lax.cond(live, update, lambda kept: kept, carried)

    peak, weight_sum, mixed_values = lax.fori_loop(0, count, tile_step, start_state)
    attended = (
        (mixed_values / weight_sum[..., None]).transpose(2, 0, 1, 3).reshape(token_rows, query_cols)
    )
    numerator = jnp.dot(attended, head_w.astype(jnp.float32), precision=lax.Precision.HIGHEST)
    squares = jnp.sum(attended * attended, axis=1)
    section = lax.axis_index("sec")
    total_num, total_sq = lax.psum((numerator, squares), "tp")
    score = total_num / jnp.sqrt(total_sq / (QUERY_HEAD_COUNT * HEAD_SIZE) + 1e-05)
    other = swapped(score, "sec", 0)
    policy = jnp.where(section == 0, score, other)
    frozen = jnp.where(section == 0, other, score)
    gap = frozen - policy
    kl_full = answer * (jnp.exp(gap) - gap - 1.0)
    objective_full = answer * advantage - BETA * kl_full
    half = token_rows // 2
    kl_term = lax.dynamic_slice_in_dim(kl_full, section * half, half, 0)
    objective = lax.dynamic_slice_in_dim(objective_full, section * half, half, 0)
    return (kl_term, objective)


def token_places(index, section, rows):
    chip = 2 * rows
    row = lax.rem(index, chip)
    return index - row + lax.rem(row + section * rows, chip)


def attention_kernel(lengths, where, block, head, out, rows):
    tokens = block.shape[0]
    section = where[0]

    def place(shape, axis):
        return token_places(lax.broadcasted_iota(jnp.int32, shape, axis), section, rows)

    wide = GROUP * HEAD_SIZE
    columns = [
        jnp.broadcast_to(head[:, cols].astype(jnp.float32), (HEAD_SIZE, HEAD_SIZE)).T[:, :1]
        for cols in (slice(at, at + HEAD_SIZE) for at in range(0, wide, HEAD_SIZE))
    ]
    query_pos = place((1, tokens), 1)
    key_pos = place((tokens, 1), 0)
    begin = jnp.zeros((1, tokens), jnp.int32)
    start = jnp.int32(0)
    for index in range(lengths.shape[0] - 1):
        start = start + lengths[index]
        begin = jnp.where(query_pos >= start, start, begin)
    valid = (key_pos <= query_pos) & (key_pos >= begin)
    key = block[:, wide : wide + HEAD_SIZE]
    value = block[:, wide + HEAD_SIZE :]
    numerator = jnp.zeros((1, tokens), jnp.float32)
    squares = jnp.zeros((1, tokens), jnp.float32)
    for index in range(GROUP):
        logits = lax.dot_general(
            key,
            block[:, index * HEAD_SIZE : (index + 1) * HEAD_SIZE],
            (((1,), (1,)), ((), ())),
            preferred_element_type=jnp.float32,
        )
        masked = jnp.where(valid, logits, NEGATIVE)
        peak = jnp.max(masked, axis=0, keepdims=True)
        weights = jnp.exp2((masked - peak) * (HEAD_SIZE ** (-0.5) * math.log2(math.e)))
        total = jnp.sum(weights, axis=0, keepdims=True)
        mixed = lax.dot_general(
            value,
            weights.astype(jnp.bfloat16),
            (((0,), (0,)), ((), ())),
            preferred_element_type=jnp.float32,
        )
        attended = mixed * (1.0 / total)
        numerator += jnp.sum(attended * columns[index], axis=0, keepdims=True)
        squares += jnp.sum(attended * attended, axis=0, keepdims=True)
    for ctx in range(tokens // (2 * rows)):
        own = slice(2 * ctx * rows, (2 * ctx + 1) * rows)
        other = slice((2 * ctx + 1) * rows, (2 * ctx + 2) * rows)
        same, cross = (
            jnp.concatenate([numerator[:, part], squares[:, part]], axis=1)
            for part in (own, other)
        )
        for core in range(2):
            row = jnp.where(section == core, same, cross)
            for share in range(2):
                out[ctx * 4 + core * 2 + share] = row


def final_kernel(lengths, prompt_len, reward, where, parts, kl_term, objective):
    rows = kl_term.shape[1]
    shares = parts.shape[0]
    scores = []
    for core in range(2):
        picked = [parts[i] for i in range(shares) if i // 2 % 2 == core]
        while len(picked) > 1:
            picked = [one + two for one, two in zip(picked[::2], picked[1::2])]
        mean_square = picked[0][:, rows:] / (QUERY_HEAD_COUNT * HEAD_SIZE)
        scores.append(picked[0][:, :rows] / jnp.sqrt(mean_square + 1e-05))
    position = (where[1] * 2 + where[0]) * rows + lax.broadcasted_iota(jnp.int32, (1, rows), 1)
    rolls = lengths.shape[0]
    mean = reward[0]
    for index in range(1, rolls):
        mean = mean + reward[index]
    mean = mean / rolls
    begin = jnp.zeros((1, rows), jnp.int32)
    prompt = jnp.zeros((1, rows), jnp.int32) + prompt_len[0]
    advantage = jnp.zeros((1, rows), jnp.float32) + (reward[0] - mean)
    start = jnp.int32(0)
    for index in range(1, rolls):
        start = start + lengths[index - 1]
        inside = position >= start
        begin = jnp.where(inside, start, begin)
        prompt = jnp.where(inside, prompt_len[index], prompt)
        advantage = jnp.where(inside, reward[index] - mean, advantage)
    answer = jnp.where(position - begin >= prompt, 1.0, 0.0)
    gap = scores[1] - scores[0]
    term = answer * (jnp.exp(gap) - gap - 1.0)
    kl_term[...] = term
    objective[...] = answer * advantage - BETA * term


def products(held, weights, low, front, store):
    wide = GROUP * HEAD_SIZE
    query_w, key_w, value_w = weights
    for turn in range(2):
        first = pl.multiple_of((low + (front ^ turn)) * wide, HEAD_SIZE)
        total = jnp.dot(
            held, query_w[0, :, pl.ds(first, wide)], preferred_element_type=jnp.float32
        )
        store(turn, 0, total * LINK_SCALE)
    for index, weight in enumerate((key_w, value_w)):
        first = pl.multiple_of(low * HEAD_SIZE, HEAD_SIZE)
        total = jnp.dot(
            held, weight[0, :, pl.ds(first, 2 * HEAD_SIZE)], preferred_element_type=jnp.float32
        )
        total = total * LINK_SCALE
        lower, upper = total[:, :HEAD_SIZE], total[:, HEAD_SIZE:]
        for turn, (one, two) in enumerate(((lower, upper), (upper, lower))):
            store(turn, wide + index * HEAD_SIZE, jnp.where(front == 0, one, two))


def cut_kernel(plan, hidden, *refs):
    outs, done = refs[:-1], refs[-1]
    copies = []
    for index, out in enumerate(outs):
        rows, depth = out.shape
        first = 0
        if rows < hidden.shape[0]:
            first = pl.multiple_of(plan[0] * rows, rows)
        start = pl.multiple_of(plan[1 + index] * depth, HEAD_SIZE)
        part = hidden.at[pl.ds(first, rows), pl.ds(start, depth)]
        copies.append(pltpu.make_async_copy(part, out, done.at[index]))
    for copy in copies:
        copy.start()
    for copy in copies:
        copy.wait()


def own_kernel(plan, own, other, query_w, key_w, value_w, out, sources):
    held = jnp.concatenate([own[...], other[...]], axis=0)
    for pair in range(2):

        def store(turn, start, total):
            out[2 * pair + turn, :, start : start + total.shape[1]] = total

        low, front = plan[sources + 2 * pair], plan[sources + 2 * pair + 1]
        products(held, (query_w, key_w, value_w), low, front, store)


def rest_kernel(plan, *refs, pair, layout):
    pieces = refs[: len(layout)]
    own, query_w, key_w, value_w, outs, tokens = refs[len(layout) :]
    chip = own.shape[1]
    sources = tokens.shape[0] // chip

    def place(slot):
        return pl.ds(pl.multiple_of(plan[slot] * chip, chip), chip)

    for piece, (base, half) in zip(pieces, layout):
        rows = piece.shape[0]
        if half is not None:
            base = pl.multiple_of(base + (plan[sources + 5] ^ half) * rows, rows)
        tokens[pl.ds(base, rows), :] = piece[...]
    for turn in range(2):
        outs[turn, place(sources), :] = own[2 * pair + turn]

    def store(turn, start, total):
        for slot in range(sources):
            part = total[slot * chip : (slot + 1) * chip, :]
            outs[turn, place(slot), start : start + total.shape[1]] = part

    low, front = plan[sources + 1 + 2 * pair], plan[sources + 2 + 2 * pair]
    products(tokens[...], (query_w, key_w, value_w), low, front, store)


def partial_call(kernel, shapes, operands, scratch, tokens, owners):
    vmem = pl.BlockSpec(memory_space=pltpu.VMEM)
    smem = pl.BlockSpec(memory_space=pltpu.SMEM)
    depth = operands[1].shape[1]
    cols = (GROUP + 2) * HEAD_SIZE
    return pl.pallas_call(
        kernel,
        out_shape=[jax.ShapeDtypeStruct(shape, jnp.float32) for shape in shapes],
        in_specs=[vmem if operand.ndim > 1 else smem for operand in operands],
        out_specs=[vmem for _ in shapes],
        scratch_shapes=scratch,
        compiler_params=pltpu.CompilerParams(vmem_limit_bytes=GRANT * 1024 * 1024),
        cost_estimate=pl.CostEstimate(
            flops=int(2 * owners * tokens * depth * cols),
            bytes_accessed=int(2 * (tokens * depth + owners * cols * (depth + 2 * tokens))),
            transcendentals=0,
        ),
    )(*operands)


def split_shards(
    hidden, w_query, key_projection, value_projection, score_head, lengths, prompt_len, reward
):
    rows = hidden.shape[0]
    depth = w_query.shape[1]
    ctx = lax.axis_index("ctx")
    section = lax.axis_index("sec")
    share = lax.axis_index("tp")
    count = 4
    f16, f32 = jnp.float16, jnp.float32

    steps = (2, 3, 1)
    half_rows = rows // 2
    targets = [(ctx + step) % count for step in (*steps, 0)]
    cuts = pl.pallas_call(
        cut_kernel,
        out_shape=[
            jax.ShapeDtypeStruct((half_rows if step == 2 else rows, depth), hidden.dtype)
            for step in (*steps, 0)
        ],
        in_specs=[
            pl.BlockSpec(memory_space=pltpu.SMEM),
            pl.BlockSpec(memory_space=pl.ANY),
        ],
        out_specs=[pl.BlockSpec(memory_space=pltpu.VMEM)] * 4,
        scratch_shapes=[pltpu.SemaphoreType.DMA((4,))],
        compiler_params=pltpu.CompilerParams(vmem_limit_bytes=4 * 1024 * 1024),
    )(jnp.stack([share, *targets]).astype(jnp.int32), hidden)
    mine = cuts[3]
    sent = {}
    for step, piece in zip(steps, cuts):
        pairs = [(i, (i + step) % count) for i in range(count)]
        sent[step] = lax.ppermute(piece, "ctx", pairs)
    weights = (w_query, key_projection, value_projection)
    cols = (GROUP + 2) * HEAD_SIZE
    chip = 2 * rows
    left = ctx < 2
    low = jnp.where(left, 2, 0)
    plan = jnp.stack(
        [*((ctx - step) % count for step in steps), ctx]
        + [low, jnp.where(left, 1, 0), 2 - low, 1 - ctx % 2, share]
    ).astype(jnp.int32)
    (own,) = partial_call(
        lambda *refs: own_kernel(*refs, sources=count),
        [(count, chip, cols)],
        (plan, mine, swapped(mine, "sec", 0), *weights),
        [],
        chip,
        count,
    )

    sent[2], own = lax.optimization_barrier((sent[2], own))
    swap = swapped(sent[2], "tp", 0)
    sent[1], sent[3], swap, own = lax.optimization_barrier((sent[1], sent[3], swap, own))
    pieces, layout = [], []
    for slot, step in enumerate(steps):
        parts = [(sent[step], None)]
        if step == 2:
            parts = [(sent[step], 0), (swap, 1)]
        for part, half in parts:
            pieces += [part, swapped(part, "sec", 0)]
            layout += [(slot * chip, half), (slot * chip + rows, half)]

    def rest(pair):
        return partial_call(
            lambda *refs: rest_kernel(*refs, pair=pair, layout=layout),
            [(2, count * chip, cols)],
            (plan, *pieces, own, *weights),
            [pltpu.VMEM((len(steps) * chip, depth), jnp.bfloat16)],
            len(steps) * chip,
            2,
        )[0]

    first = rest(0)
    second = rest(1)

    def reduced(first, second):
        far, first = lax.optimization_barrier((first[0].astype(f16), first))
        fold = lax.ppermute(far, "ctx", [(0, 1), (3, 2)])
        inner = first[1].astype(f16)
        middle = lax.ppermute(inner, "ctx", [(1, 2), (2, 1)])
        skip = lax.ppermute(inner, "ctx", [(0, 2), (3, 1)])
        folded = (first[0] + fold.astype(f32)).astype(f16)
        ends = lax.ppermute(folded, "ctx", [(1, 3), (2, 0)])
        beside, _ = lax.optimization_barrier((second[0].astype(f16), folded))
        near = lax.ppermute(beside, "ctx", [(0, 1), (1, 0), (2, 3), (3, 2)])
        total = second[1] + middle.astype(f32) + skip.astype(f32)
        total, near = lax.optimization_barrier((total, near))
        total, ends = lax.optimization_barrier((total + near.astype(f32), ends))
        total = total + ends.astype(f32)
        return (total * (1.0 / LINK_SCALE)).astype(jnp.bfloat16)

    mine = reduced(first, second)
    wide = GROUP * HEAD_SIZE
    smem = pl.BlockSpec(memory_space=pltpu.SMEM)
    where = jnp.stack([section, ctx]).astype(jnp.int32)
    sums = pl.pallas_call(
        lambda plan, *refs: attention_kernel(*refs, rows),
        out_shape=jax.ShapeDtypeStruct((4 * count, 1, 2 * rows), f32),
        grid_spec=pltpu.PrefetchScalarGridSpec(
            num_scalar_prefetch=1,
            grid=(1,),
            in_specs=[
                smem,
                smem,
                pl.BlockSpec(mine.shape, lambda i, plan: (0, 0)),
                pl.BlockSpec((1, wide), lambda i, plan: (0, plan[1])),
            ],
            out_specs=pl.BlockSpec((4 * count, 1, 2 * rows), lambda i, plan: (0, 0, 0)),
        ),
        compiler_params=pltpu.CompilerParams(vmem_limit_bytes=12 * 1024 * 1024),
    )(where, lengths, where, mine, score_head)

    spread = lax.all_to_all(sums, ("ctx", "sec", "tp"), 0, 0, tiled=True)
    vmem = pl.BlockSpec(memory_space=pltpu.VMEM)
    kl_term, objective = pl.pallas_call(
        final_kernel,
        out_shape=[jax.ShapeDtypeStruct((1, rows), f32)] * 2,
        in_specs=[smem, smem, smem, smem, vmem],
        out_specs=[vmem, vmem],
        compiler_params=pltpu.CompilerParams(vmem_limit_bytes=4 * 1024 * 1024),
    )(lengths, prompt_len, reward, where, spread)
    return (kl_term.reshape(rows), objective.reshape(rows))


def solution(mesh):
    placed = (
        P(("grp", "ctx", "sec"), None),
        P("sec", "ctx", "tp"),
        P("sec", "ctx", "tp"),
        P("sec", "ctx", "tp"),
        P("sec", "tp"),
        P("grp"),
        P("grp"),
        P("grp"),
    )
    own_heads = KEY_VALUE_HEADS // mesh.shape["tp"]
    by_heads = mesh.shape["ctx"] == 4 and own_heads == 4
    return jax.shard_map(
        split_shards if by_heads else gathered_shards,
        mesh=mesh,
        in_specs=placed,
        out_specs=(P(("grp", "ctx", "sec")), P(("grp", "ctx", "sec"))),
        check_vma=False,
    )
```

```python
import math

import jax
import jax.numpy as jnp
from jax import lax
from jax.experimental import pallas as pl
from jax.experimental.pallas import tpu as pltpu
from jax.sharding import PartitionSpec as P

QUERY_HEAD_COUNT = 32
KEY_VALUE_HEADS = 8
HEAD_SIZE = 128


BETA = 0.1
NEGATIVE = -1e30
LINK_SCALE = 16.0
GROUP = QUERY_HEAD_COUNT // KEY_VALUE_HEADS
GRANT = 12


def swapped(array, axis, distance):
    return lax.ppermute(array, axis, [(i, i ^ 1 << distance) for i in range(lax.axis_size(axis))])


def rollout_tables(lengths, prompt_len, reward, position):
    starts = jnp.cumsum(lengths) - lengths
    inside = starts[None, :] <= position[:, None]
    begin = jnp.max(jnp.where(inside, starts[None, :], 0), axis=1)
    latest = jnp.sum(inside.astype(jnp.int32), axis=1) - 1
    chosen = jnp.arange(lengths.shape[0], dtype=jnp.int32)[None, :] == latest[:, None]
    prompt = jnp.sum(jnp.where(chosen, prompt_len[None, :], 0), axis=1)
    centred = reward - jnp.mean(reward)
    advantage = jnp.sum(
        jnp.where(chosen, centred[None, :], jnp.zeros_like(centred)[None, :]), axis=1
    )
    answer = (position - begin >= prompt).astype(reward.dtype)
    return (begin, answer, advantage)


def gathered_shards(
    hidden, w_query, key_projection, value_projection, score_head, lengths, prompt_len, reward
):
    row_block = lax.all_gather(hidden, "sec", axis=0, tiled=True)
    token_rows = row_block.shape[0]
    query_w = w_query[0]
    key_w = key_projection[0]
    value_w = value_projection[0]
    head_w = score_head[0]
    query_cols = query_w.shape[1]
    pair_cols = key_w.shape[1]

    def add_rows(piece):
        return jnp.dot(row_block, piece, preferred_element_type=jnp.float32)

    query_rows = add_rows(lax.all_gather(query_w, "ctx", axis=0, tiled=True))
    key_rows = add_rows(lax.all_gather(key_w, "ctx", axis=0, tiled=True))
    value_rows = add_rows(lax.all_gather(value_w, "ctx", axis=0, tiled=True))
    query_rows = query_rows.astype(jnp.bfloat16)
    key_rows = key_rows.astype(jnp.bfloat16)
    value_rows = value_rows.astype(jnp.bfloat16)
    heads_here = pair_cols // HEAD_SIZE
    score_scale = HEAD_SIZE ** (-0.5)
    row_pos = lax.axis_index("ctx") * token_rows + jnp.arange(token_rows, dtype=jnp.int32)
    begin, answer, advantage = rollout_tables(lengths, prompt_len, reward, row_pos)
    first_begin = jnp.min(begin)
    last_row = row_pos[token_rows - 1]
    query_heads = query_rows.reshape(token_rows, heads_here, GROUP, HEAD_SIZE)
    start_state = (
        jnp.full((heads_here, GROUP, token_rows), NEGATIVE, jnp.float32),
        jnp.zeros((heads_here, GROUP, token_rows), jnp.float32),
        jnp.zeros((heads_here, GROUP, token_rows, HEAD_SIZE), jnp.float32),
    )
    key_piece = lax.all_gather(key_rows, "ctx", axis=0, tiled=True)
    value_piece = lax.all_gather(value_rows, "ctx", axis=0, tiled=True)
    count = key_piece.shape[0] // token_rows

    def tile_step(index, carried):
        offset = index * token_rows
        key_tile = lax.dynamic_slice_in_dim(key_piece, offset, token_rows, 0).reshape(
            token_rows, heads_here, HEAD_SIZE
        )
        value_tile = lax.dynamic_slice_in_dim(value_piece, offset, token_rows, 0).reshape(
            token_rows, heads_here, HEAD_SIZE
        )
        key_pos = offset + jnp.arange(token_rows, dtype=jnp.int32)

        def update(current):
            peak, weight_sum, mixed_values = current
            score_logits = (
                jnp.einsum(
                    "rkgd,pkd->kgrp", query_heads, key_tile, preferred_element_type=jnp.float32
                )
                * score_scale
            )
            valid = (key_pos[None, :] <= row_pos[:, None]) & (key_pos[None, :] >= begin[:, None])
            masked = jnp.where(valid[None, None], score_logits, NEGATIVE)
            new_peak = jnp.maximum(peak, jnp.max(masked, axis=3))
            weights = jnp.where(
                valid[None, None],
                jnp.exp(score_logits - new_peak[..., None]),
                jnp.zeros_like(score_logits),
            )
            factor = jnp.exp(peak - new_peak)
            new_sum = weight_sum * factor + jnp.sum(weights, axis=3)
            product = jnp.einsum(
                "kgrp,pkd->kgrd",
                weights.astype(jnp.bfloat16),
                value_tile,
                preferred_element_type=jnp.float32,
            )
            return (new_peak, new_sum, mixed_values * factor[..., None] + product)

        live = (offset <= last_row) & (offset + token_rows - 1 >= first_begin)
        return lax.cond(live, update, lambda kept: kept, carried)

    peak, weight_sum, mixed_values = lax.fori_loop(0, count, tile_step, start_state)
    attended = (
        (mixed_values / weight_sum[..., None]).transpose(2, 0, 1, 3).reshape(token_rows, query_cols)
    )
    numerator = jnp.dot(attended, head_w.astype(jnp.float32), precision=lax.Precision.HIGHEST)
    squares = jnp.sum(attended * attended, axis=1)
    section = lax.axis_index("sec")
    total_num, total_sq = lax.psum((numerator, squares), "tp")
    score = total_num / jnp.sqrt(total_sq / (QUERY_HEAD_COUNT * HEAD_SIZE) + 1e-05)
    other = swapped(score, "sec", 0)
    policy = jnp.where(section == 0, score, other)
    frozen = jnp.where(section == 0, other, score)
    gap = frozen - policy
    kl_full = answer * (jnp.exp(gap) - gap - 1.0)
    objective_full = answer * advantage - BETA * kl_full
    half = token_rows // 2
    kl_term = lax.dynamic_slice_in_dim(kl_full, section * half, half, 0)
    objective = lax.dynamic_slice_in_dim(objective_full, section * half, half, 0)
    return (kl_term, objective)


def token_places(index, section, rows):
    chip = 2 * rows
    row = lax.rem(index, chip)
    return index - row + lax.rem(row + section * rows, chip)


def attention_kernel(lengths, where, block, head, out, rows):
    tokens = block.shape[0]
    section = where[0]

    def place(shape, axis):
        return token_places(lax.broadcasted_iota(jnp.int32, shape, axis), section, rows)

    wide = GROUP * HEAD_SIZE
    columns = [
        jnp.broadcast_to(head[:, cols].astype(jnp.float32), (HEAD_SIZE, HEAD_SIZE)).T[:, :1]
        for cols in (slice(at, at + HEAD_SIZE) for at in range(0, wide, HEAD_SIZE))
    ]
    query_pos = place((1, tokens), 1)
    key_pos = place((tokens, 1), 0)
    begin = jnp.zeros((1, tokens), jnp.int32)
    start = jnp.int32(0)
    for index in range(lengths.shape[0] - 1):
        start = start + lengths[index]
        begin = jnp.where(query_pos >= start, start, begin)
    valid = (key_pos <= query_pos) & (key_pos >= begin)
    key = block[:, wide : wide + HEAD_SIZE]
    value = block[:, wide + HEAD_SIZE :]
    numerator = jnp.zeros((1, tokens), jnp.float32)
    squares = jnp.zeros((1, tokens), jnp.float32)
    for index in range(GROUP):
        logits = lax.dot_general(
            key,
            block[:, index * HEAD_SIZE : (index + 1) * HEAD_SIZE],
            (((1,), (1,)), ((), ())),
            preferred_element_type=jnp.float32,
        )
        masked = jnp.where(valid, logits, NEGATIVE)
        peak = jnp.max(masked, axis=0, keepdims=True)
        weights = jnp.exp2((masked - peak) * (HEAD_SIZE ** (-0.5) * math.log2(math.e)))
        total = jnp.sum(weights, axis=0, keepdims=True)
        mixed = lax.dot_general(
            value,
            weights.astype(jnp.bfloat16),
            (((0,), (0,)), ((), ())),
            preferred_element_type=jnp.float32,
        )
        attended = mixed * (1.0 / total)
        numerator += jnp.sum(attended * columns[index], axis=0, keepdims=True)
        squares += jnp.sum(attended * attended, axis=0, keepdims=True)
    for ctx in range(tokens // (2 * rows)):
        own = slice(2 * ctx * rows, (2 * ctx + 1) * rows)
        other = slice((2 * ctx + 1) * rows, (2 * ctx + 2) * rows)
        same, cross = (
            jnp.concatenate([numerator[:, part], squares[:, part]], axis=1)
            for part in (own, other)
        )
        for core in range(2):
            row = jnp.where(section == core, same, cross)
            for share in range(2):
                out[ctx * 4 + core * 2 + share] = row


def final_kernel(lengths, prompt_len, reward, where, parts, kl_term, objective):
    rows = kl_term.shape[1]
    shares = parts.shape[0]
    scores = []
    for core in range(2):
        picked = [parts[i] for i in range(shares) if i // 2 % 2 == core]
        while len(picked) > 1:
            picked = [one + two for one, two in zip(picked[::2], picked[1::2])]
        mean_square = picked[0][:, rows:] / (QUERY_HEAD_COUNT * HEAD_SIZE)
        scores.append(picked[0][:, :rows] / jnp.sqrt(mean_square + 1e-05))
    position = (where[1] * 2 + where[0]) * rows + lax.broadcasted_iota(jnp.int32, (1, rows), 1)
    rolls = lengths.shape[0]
    mean = reward[0]
    for index in range(1, rolls):
        mean = mean + reward[index]
    mean = mean / rolls
    begin = jnp.zeros((1, rows), jnp.int32)
    prompt = jnp.zeros((1, rows), jnp.int32) + prompt_len[0]
    advantage = jnp.zeros((1, rows), jnp.float32) + (reward[0] - mean)
    start = jnp.int32(0)
    for index in range(1, rolls):
        start = start + lengths[index - 1]
        inside = position >= start
        begin = jnp.where(inside, start, begin)
        prompt = jnp.where(inside, prompt_len[index], prompt)
        advantage = jnp.where(inside, reward[index] - mean, advantage)
    answer = jnp.where(position - begin >= prompt, 1.0, 0.0)
    gap = scores[1] - scores[0]
    term = answer * (jnp.exp(gap) - gap - 1.0)
    kl_term[...] = term
    objective[...] = answer * advantage - BETA * term


def products(held, weights, low, front, store):
    wide = GROUP * HEAD_SIZE
    query_w, key_w, value_w = weights
    for turn in range(2):
        first = pl.multiple_of((low + (front ^ turn)) * wide, HEAD_SIZE)
        total = jnp.dot(
            held, query_w[0, :, pl.ds(first, wide)], preferred_element_type=jnp.float32
        )
        store(turn, 0, total * LINK_SCALE)
    for index, weight in enumerate((key_w, value_w)):
        first = pl.multiple_of(low * HEAD_SIZE, HEAD_SIZE)
        total = jnp.dot(
            held, weight[0, :, pl.ds(first, 2 * HEAD_SIZE)], preferred_element_type=jnp.float32
        )
        total = total * LINK_SCALE
        lower, upper = total[:, :HEAD_SIZE], total[:, HEAD_SIZE:]
        for turn, (one, two) in enumerate(((lower, upper), (upper, lower))):
            store(turn, wide + index * HEAD_SIZE, jnp.where(front == 0, one, two))


def cut_kernel(plan, hidden, *refs):
    outs, done = refs[:-1], refs[-1]
    copies = []
    for index, out in enumerate(outs):
        rows, depth = out.shape
        first = 0
        if rows < hidden.shape[0]:
            first = pl.multiple_of(plan[0] * rows, rows)
        start = pl.multiple_of(plan[1 + index] * depth, HEAD_SIZE)
        part = hidden.at[pl.ds(first, rows), pl.ds(start, depth)]
        copies.append(pltpu.make_async_copy(part, out, done.at[index]))
    for copy in copies:
        copy.start()
    for copy in copies:
        copy.wait()


def own_kernel(plan, own, other, query_w, key_w, value_w, out, sources):
    held = jnp.concatenate([own[...], other[...]], axis=0)
    for pair in range(2):

        def store(turn, start, total):
            out[2 * pair + turn, :, start : start + total.shape[1]] = total

        low, front = plan[sources + 2 * pair], plan[sources + 2 * pair + 1]
        products(held, (query_w, key_w, value_w), low, front, store)


def rest_kernel(plan, *refs, pair, layout):
    pieces = refs[: len(layout)]
    own, query_w, key_w, value_w, outs, tokens = refs[len(layout) :]
    chip = own.shape[1]
    sources = tokens.shape[0] // chip

    def place(slot):
        return pl.ds(pl.multiple_of(plan[slot] * chip, chip), chip)

    for piece, (base, half) in zip(pieces, layout):
        rows = piece.shape[0]
        if half is not None:
            base = pl.multiple_of(base + (plan[sources + 5] ^ half) * rows, rows)
        tokens[pl.ds(base, rows), :] = piece[...]
    for turn in range(2):
        outs[turn, place(sources), :] = own[2 * pair + turn]

    def store(turn, start, total):
        for slot in range(sources):
            part = total[slot * chip : (slot + 1) * chip, :]
            outs[turn, place(slot), start : start + total.shape[1]] = part

    low, front = plan[sources + 1 + 2 * pair], plan[sources + 2 + 2 * pair]
    products(tokens[...], (query_w, key_w, value_w), low, front, store)


def partial_call(kernel, shapes, operands, scratch, tokens, owners):
    vmem = pl.BlockSpec(memory_space=pltpu.VMEM)
    smem = pl.BlockSpec(memory_space=pltpu.SMEM)
    depth = operands[1].shape[1]
    cols = (GROUP + 2) * HEAD_SIZE
    return pl.pallas_call(
        kernel,
        out_shape=[jax.ShapeDtypeStruct(shape, jnp.float32) for shape in shapes],
        in_specs=[vmem if operand.ndim > 1 else smem for operand in operands],
        out_specs=[vmem for _ in shapes],
        scratch_shapes=scratch,
        compiler_params=pltpu.CompilerParams(vmem_limit_bytes=GRANT * 1024 * 1024),
        cost_estimate=pl.CostEstimate(
            flops=int(2 * owners * tokens * depth * cols),
            bytes_accessed=int(2 * (tokens * depth + owners * cols * (depth + 2 * tokens))),
            transcendentals=0,
        ),
    )(*operands)


def split_shards(
    hidden, w_query, key_projection, value_projection, score_head, lengths, prompt_len, reward
):
    rows = hidden.shape[0]
    depth = w_query.shape[1]
    ctx = lax.axis_index("ctx")
    section = lax.axis_index("sec")
    share = lax.axis_index("tp")
    count = 4
    f16, f32 = jnp.float16, jnp.float32

    steps = (2, 3, 1)
    half_rows = rows // 2
    targets = [(ctx + step) % count for step in (*steps, 0)]
    cuts = pl.pallas_call(
        cut_kernel,
        out_shape=[
            jax.ShapeDtypeStruct((half_rows if step == 2 else rows, depth), hidden.dtype)
            for step in (*steps, 0)
        ],
        in_specs=[
            pl.BlockSpec(memory_space=pltpu.SMEM),
            pl.BlockSpec(memory_space=pl.ANY),
        ],
        out_specs=[pl.BlockSpec(memory_space=pltpu.VMEM)] * 4,
        scratch_shapes=[pltpu.SemaphoreType.DMA((4,))],
        compiler_params=pltpu.CompilerParams(vmem_limit_bytes=4 * 1024 * 1024),
    )(jnp.stack([share, *targets]).astype(jnp.int32), hidden)
    mine = cuts[3]
    sent = {}
    for step, piece in zip(steps, cuts):
        pairs = [(i, (i + step) % count) for i in range(count)]
        sent[step] = lax.ppermute(piece, "ctx", pairs)
    weights = (w_query, key_projection, value_projection)
    cols = (GROUP + 2) * HEAD_SIZE
    chip = 2 * rows
    left = ctx < 2
    low = jnp.where(left, 2, 0)
    plan = jnp.stack(
        [*((ctx - step) % count for step in steps), ctx]
        + [low, jnp.where(left, 1, 0), 2 - low, 1 - ctx % 2, share]
    ).astype(jnp.int32)
    (own,) = partial_call(
        lambda *refs: own_kernel(*refs, sources=count),
        [(count, chip, cols)],
        (plan, mine, swapped(mine, "sec", 0), *weights),
        [],
        chip,
        count,
    )

    sent[2], own = lax.optimization_barrier((sent[2], own))
    swap = swapped(sent[2], "tp", 0)
    sent[1], sent[3], swap, own = lax.optimization_barrier((sent[1], sent[3], swap, own))
    pieces, layout = [], []
    for slot, step in enumerate(steps):
        parts = [(sent[step], None)]
        if step == 2:
            parts = [(sent[step], 0), (swap, 1)]
        for part, half in parts:
            pieces += [part, swapped(part, "sec", 0)]
            layout += [(slot * chip, half), (slot * chip + rows, half)]

    def rest(pair):
        return partial_call(
            lambda *refs: rest_kernel(*refs, pair=pair, layout=layout),
            [(2, count * chip, cols)],
            (plan, *pieces, own, *weights),
            [pltpu.VMEM((len(steps) * chip, depth), jnp.bfloat16)],
            len(steps) * chip,
            2,
        )[0]

    first = rest(0)
    second = rest(1)

    def reduced(first, second):
        far = first[0].astype(f16)
        fold = lax.ppermute(far, "ctx", [(0, 1), (3, 2)])
        inner = first[1].astype(f16)
        middle = lax.ppermute(inner, "ctx", [(1, 2), (2, 1)])
        skip = lax.ppermute(inner, "ctx", [(0, 2), (3, 1)])
        folded = (first[0] + fold.astype(f32)).astype(f16)
        ends = lax.ppermute(folded, "ctx", [(1, 3), (2, 0)])
        beside, _ = lax.optimization_barrier((second[0].astype(f16), folded))
        near = lax.ppermute(beside, "ctx", [(0, 1), (1, 0), (2, 3), (3, 2)])
        total = second[1] + middle.astype(f32) + skip.astype(f32)
        total, near = lax.optimization_barrier((total, near))
        total, ends = lax.optimization_barrier((total + near.astype(f32), ends))
        total = total + ends.astype(f32)
        return (total * (1.0 / LINK_SCALE)).astype(jnp.bfloat16)

    mine = reduced(first, second)
    wide = GROUP * HEAD_SIZE
    smem = pl.BlockSpec(memory_space=pltpu.SMEM)
    where = jnp.stack([section, ctx]).astype(jnp.int32)
    sums = pl.pallas_call(
        lambda plan, *refs: attention_kernel(*refs, rows),
        out_shape=jax.ShapeDtypeStruct((4 * count, 1, 2 * rows), f32),
        grid_spec=pltpu.PrefetchScalarGridSpec(
            num_scalar_prefetch=1,
            grid=(1,),
            in_specs=[
                smem,
                smem,
                pl.BlockSpec(mine.shape, lambda i, plan: (0, 0)),
                pl.BlockSpec((1, wide), lambda i, plan: (0, plan[1])),
            ],
            out_specs=pl.BlockSpec((4 * count, 1, 2 * rows), lambda i, plan: (0, 0, 0)),
        ),
        compiler_params=pltpu.CompilerParams(vmem_limit_bytes=12 * 1024 * 1024),
    )(where, lengths, where, mine, score_head)

    spread = lax.all_to_all(sums, ("ctx", "sec", "tp"), 0, 0, tiled=True)
    vmem = pl.BlockSpec(memory_space=pltpu.VMEM)
    kl_term, objective = pl.pallas_call(
        final_kernel,
        out_shape=[jax.ShapeDtypeStruct((1, rows), f32)] * 2,
        in_specs=[smem, smem, smem, smem, vmem],
        out_specs=[vmem, vmem],
        compiler_params=pltpu.CompilerParams(vmem_limit_bytes=4 * 1024 * 1024),
    )(lengths, prompt_len, reward, where, spread)
    return (kl_term.reshape(rows), objective.reshape(rows))


def solution(mesh):
    placed = (
        P(("grp", "ctx", "sec"), None),
        P("sec", "ctx", "tp"),
        P("sec", "ctx", "tp"),
        P("sec", "ctx", "tp"),
        P("sec", "tp"),
        P("grp"),
        P("grp"),
        P("grp"),
    )
    own_heads = KEY_VALUE_HEADS // mesh.shape["tp"]
    by_heads = mesh.shape["ctx"] == 4 and own_heads == 4
    return jax.shard_map(
        split_shards if by_heads else gathered_shards,
        mesh=mesh,
        in_specs=placed,
        out_specs=(P(("grp", "ctx", "sec")), P(("grp", "ctx", "sec"))),
        check_vma=False,
    )
```

```python
import math

import jax
import jax.numpy as jnp
from jax import lax
from jax.experimental import pallas as pl
from jax.experimental.pallas import tpu as pltpu
from jax.sharding import PartitionSpec as P

QUERY_HEAD_COUNT = 32
KEY_VALUE_HEADS = 8
HEAD_SIZE = 128


BETA = 0.1
NEGATIVE = -1e30
LINK_SCALE = 16.0
GROUP = QUERY_HEAD_COUNT // KEY_VALUE_HEADS
GRANT = 12


def swapped(array, axis, distance):
    return lax.ppermute(array, axis, [(i, i ^ 1 << distance) for i in range(lax.axis_size(axis))])


def rollout_tables(lengths, prompt_len, reward, position):
    starts = jnp.cumsum(lengths) - lengths
    inside = starts[None, :] <= position[:, None]
    begin = jnp.max(jnp.where(inside, starts[None, :], 0), axis=1)
    latest = jnp.sum(inside.astype(jnp.int32), axis=1) - 1
    chosen = jnp.arange(lengths.shape[0], dtype=jnp.int32)[None, :] == latest[:, None]
    prompt = jnp.sum(jnp.where(chosen, prompt_len[None, :], 0), axis=1)
    centred = reward - jnp.mean(reward)
    advantage = jnp.sum(
        jnp.where(chosen, centred[None, :], jnp.zeros_like(centred)[None, :]), axis=1
    )
    answer = (position - begin >= prompt).astype(reward.dtype)
    return (begin, answer, advantage)


def gathered_shards(
    hidden, w_query, key_projection, value_projection, score_head, lengths, prompt_len, reward
):
    row_block = lax.all_gather(hidden, "sec", axis=0, tiled=True)
    token_rows = row_block.shape[0]
    query_w = w_query[0]
    key_w = key_projection[0]
    value_w = value_projection[0]
    head_w = score_head[0]
    query_cols = query_w.shape[1]
    pair_cols = key_w.shape[1]

    def add_rows(piece):
        return jnp.dot(row_block, piece, preferred_element_type=jnp.float32)

    query_rows = add_rows(lax.all_gather(query_w, "ctx", axis=0, tiled=True))
    key_rows = add_rows(lax.all_gather(key_w, "ctx", axis=0, tiled=True))
    value_rows = add_rows(lax.all_gather(value_w, "ctx", axis=0, tiled=True))
    query_rows = query_rows.astype(jnp.bfloat16)
    key_rows = key_rows.astype(jnp.bfloat16)
    value_rows = value_rows.astype(jnp.bfloat16)
    heads_here = pair_cols // HEAD_SIZE
    score_scale = HEAD_SIZE ** (-0.5)
    row_pos = lax.axis_index("ctx") * token_rows + jnp.arange(token_rows, dtype=jnp.int32)
    begin, answer, advantage = rollout_tables(lengths, prompt_len, reward, row_pos)
    first_begin = jnp.min(begin)
    last_row = row_pos[token_rows - 1]
    query_heads = query_rows.reshape(token_rows, heads_here, GROUP, HEAD_SIZE)
    start_state = (
        jnp.full((heads_here, GROUP, token_rows), NEGATIVE, jnp.float32),
        jnp.zeros((heads_here, GROUP, token_rows), jnp.float32),
        jnp.zeros((heads_here, GROUP, token_rows, HEAD_SIZE), jnp.float32),
    )
    key_piece = lax.all_gather(key_rows, "ctx", axis=0, tiled=True)
    value_piece = lax.all_gather(value_rows, "ctx", axis=0, tiled=True)
    count = key_piece.shape[0] // token_rows

    def tile_step(index, carried):
        offset = index * token_rows
        key_tile = lax.dynamic_slice_in_dim(key_piece, offset, token_rows, 0).reshape(
            token_rows, heads_here, HEAD_SIZE
        )
        value_tile = lax.dynamic_slice_in_dim(value_piece, offset, token_rows, 0).reshape(
            token_rows, heads_here, HEAD_SIZE
        )
        key_pos = offset + jnp.arange(token_rows, dtype=jnp.int32)

        def update(current):
            peak, weight_sum, mixed_values = current
            score_logits = (
                jnp.einsum(
                    "rkgd,pkd->kgrp", query_heads, key_tile, preferred_element_type=jnp.float32
                )
                * score_scale
            )
            valid = (key_pos[None, :] <= row_pos[:, None]) & (key_pos[None, :] >= begin[:, None])
            masked = jnp.where(valid[None, None], score_logits, NEGATIVE)
            new_peak = jnp.maximum(peak, jnp.max(masked, axis=3))
            weights = jnp.where(
                valid[None, None],
                jnp.exp(score_logits - new_peak[..., None]),
                jnp.zeros_like(score_logits),
            )
            factor = jnp.exp(peak - new_peak)
            new_sum = weight_sum * factor + jnp.sum(weights, axis=3)
            product = jnp.einsum(
                "kgrp,pkd->kgrd",
                weights.astype(jnp.bfloat16),
                value_tile,
                preferred_element_type=jnp.float32,
            )
            return (new_peak, new_sum, mixed_values * factor[..., None] + product)

        live = (offset <= last_row) & (offset + token_rows - 1 >= first_begin)
        return lax.cond(live, update, lambda kept: kept, carried)

    peak, weight_sum, mixed_values = lax.fori_loop(0, count, tile_step, start_state)
    attended = (
        (mixed_values / weight_sum[..., None]).transpose(2, 0, 1, 3).reshape(token_rows, query_cols)
    )
    numerator = jnp.dot(attended, head_w.astype(jnp.float32), precision=lax.Precision.HIGHEST)
    squares = jnp.sum(attended * attended, axis=1)
    section = lax.axis_index("sec")
    total_num, total_sq = lax.psum((numerator, squares), "tp")
    score = total_num / jnp.sqrt(total_sq / (QUERY_HEAD_COUNT * HEAD_SIZE) + 1e-05)
    other = swapped(score, "sec", 0)
    policy = jnp.where(section == 0, score, other)
    frozen = jnp.where(section == 0, other, score)
    gap = frozen - policy
    kl_full = answer * (jnp.exp(gap) - gap - 1.0)
    objective_full = answer * advantage - BETA * kl_full
    half = token_rows // 2
    kl_term = lax.dynamic_slice_in_dim(kl_full, section * half, half, 0)
    objective = lax.dynamic_slice_in_dim(objective_full, section * half, half, 0)
    return (kl_term, objective)


def token_places(index, section, rows):
    chip = 2 * rows
    row = lax.rem(index, chip)
    return index - row + lax.rem(row + section * rows, chip)


def attention_kernel(lengths, where, block, head, out, rows):
    tokens = block.shape[0]
    section = where[0]

    def place(shape, axis):
        return token_places(lax.broadcasted_iota(jnp.int32, shape, axis), section, rows)

    wide = GROUP * HEAD_SIZE
    columns = [
        jnp.broadcast_to(head[:, cols].astype(jnp.float32), (HEAD_SIZE, HEAD_SIZE)).T[:, :1]
        for cols in (slice(at, at + HEAD_SIZE) for at in range(0, wide, HEAD_SIZE))
    ]
    query_pos = place((1, tokens), 1)
    key_pos = place((tokens, 1), 0)
    begin = jnp.zeros((1, tokens), jnp.int32)
    start = jnp.int32(0)
    for index in range(lengths.shape[0] - 1):
        start = start + lengths[index]
        begin = jnp.where(query_pos >= start, start, begin)
    valid = (key_pos <= query_pos) & (key_pos >= begin)
    key = block[:, wide : wide + HEAD_SIZE]
    value = block[:, wide + HEAD_SIZE :]
    numerator = jnp.zeros((1, tokens), jnp.float32)
    squares = jnp.zeros((1, tokens), jnp.float32)
    for index in range(GROUP):
        logits = lax.dot_general(
            key,
            block[:, index * HEAD_SIZE : (index + 1) * HEAD_SIZE],
            (((1,), (1,)), ((), ())),
            preferred_element_type=jnp.float32,
        )
        masked = jnp.where(valid, logits, NEGATIVE)
        peak = jnp.max(masked, axis=0, keepdims=True)
        weights = jnp.exp2((masked - peak) * (HEAD_SIZE ** (-0.5) * math.log2(math.e)))
        total = jnp.sum(weights, axis=0, keepdims=True)
        mixed = lax.dot_general(
            value,
            weights.astype(jnp.bfloat16),
            (((0,), (0,)), ((), ())),
            preferred_element_type=jnp.float32,
        )
        attended = mixed * (1.0 / total)
        numerator += jnp.sum(attended * columns[index], axis=0, keepdims=True)
        squares += jnp.sum(attended * attended, axis=0, keepdims=True)
    for ctx in range(tokens // (2 * rows)):
        own = slice(2 * ctx * rows, (2 * ctx + 1) * rows)
        other = slice((2 * ctx + 1) * rows, (2 * ctx + 2) * rows)
        same, cross = (
            jnp.concatenate([numerator[:, part], squares[:, part]], axis=1)
            for part in (own, other)
        )
        for core in range(2):
            row = jnp.where(section == core, same, cross)
            for share in range(2):
                out[ctx * 4 + core * 2 + share] = row


def final_kernel(lengths, prompt_len, reward, where, parts, kl_term, objective):
    rows = kl_term.shape[1]
    shares = parts.shape[0]
    scores = []
    for core in range(2):
        picked = [parts[i] for i in range(shares) if i // 2 % 2 == core]
        while len(picked) > 1:
            picked = [one + two for one, two in zip(picked[::2], picked[1::2])]
        mean_square = picked[0][:, rows:] / (QUERY_HEAD_COUNT * HEAD_SIZE)
        scores.append(picked[0][:, :rows] / jnp.sqrt(mean_square + 1e-05))
    position = (where[1] * 2 + where[0]) * rows + lax.broadcasted_iota(jnp.int32, (1, rows), 1)
    rolls = lengths.shape[0]
    mean = reward[0]
    for index in range(1, rolls):
        mean = mean + reward[index]
    mean = mean / rolls
    begin = jnp.zeros((1, rows), jnp.int32)
    prompt = jnp.zeros((1, rows), jnp.int32) + prompt_len[0]
    advantage = jnp.zeros((1, rows), jnp.float32) + (reward[0] - mean)
    start = jnp.int32(0)
    for index in range(1, rolls):
        start = start + lengths[index - 1]
        inside = position >= start
        begin = jnp.where(inside, start, begin)
        prompt = jnp.where(inside, prompt_len[index], prompt)
        advantage = jnp.where(inside, reward[index] - mean, advantage)
    answer = jnp.where(position - begin >= prompt, 1.0, 0.0)
    gap = scores[1] - scores[0]
    term = answer * (jnp.exp(gap) - gap - 1.0)
    kl_term[...] = term
    objective[...] = answer * advantage - BETA * term


def products(held, weights, low, front, store):
    wide = GROUP * HEAD_SIZE
    query_w, key_w, value_w = weights
    for turn in range(2):
        first = pl.multiple_of((low + (front ^ turn)) * wide, HEAD_SIZE)
        total = jnp.dot(
            held, query_w[0, :, pl.ds(first, wide)], preferred_element_type=jnp.float32
        )
        store(turn, 0, total * LINK_SCALE)
    for index, weight in enumerate((key_w, value_w)):
        first = pl.multiple_of(low * HEAD_SIZE, HEAD_SIZE)
        total = jnp.dot(
            held, weight[0, :, pl.ds(first, 2 * HEAD_SIZE)], preferred_element_type=jnp.float32
        )
        total = total * LINK_SCALE
        lower, upper = total[:, :HEAD_SIZE], total[:, HEAD_SIZE:]
        for turn, (one, two) in enumerate(((lower, upper), (upper, lower))):
            store(turn, wide + index * HEAD_SIZE, jnp.where(front == 0, one, two))


def cut_kernel(plan, hidden, *refs):
    outs, done = refs[:-1], refs[-1]
    copies = []
    for index, out in enumerate(outs):
        rows, depth = out.shape
        first = 0
        if rows < hidden.shape[0]:
            first = pl.multiple_of(plan[0] * rows, rows)
        start = pl.multiple_of(plan[1 + index] * depth, HEAD_SIZE)
        part = hidden.at[pl.ds(first, rows), pl.ds(start, depth)]
        copies.append(pltpu.make_async_copy(part, out, done.at[index]))
    for copy in copies:
        copy.start()
    for copy in copies:
        copy.wait()


def own_kernel(plan, own, other, query_w, key_w, value_w, out, sources):
    held = jnp.concatenate([own[...], other[...]], axis=0)
    for pair in range(2):

        def store(turn, start, total):
            out[2 * pair + turn, :, start : start + total.shape[1]] = total

        low, front = plan[sources + 2 * pair], plan[sources + 2 * pair + 1]
        products(held, (query_w, key_w, value_w), low, front, store)


def rest_kernel(plan, *refs, pair, layout):
    pieces = refs[: len(layout)]
    own, query_w, key_w, value_w, outs, tokens = refs[len(layout) :]
    chip = own.shape[1]
    sources = tokens.shape[0] // chip

    def place(slot):
        return pl.ds(pl.multiple_of(plan[slot] * chip, chip), chip)

    for piece, (base, half) in zip(pieces, layout):
        rows = piece.shape[0]
        if half is not None:
            base = pl.multiple_of(base + (plan[sources + 5] ^ half) * rows, rows)
        tokens[pl.ds(base, rows), :] = piece[...]
    for turn in range(2):
        outs[turn, place(sources), :] = own[2 * pair + turn]

    def store(turn, start, total):
        for slot in range(sources):
            part = total[slot * chip : (slot + 1) * chip, :]
            outs[turn, place(slot), start : start + total.shape[1]] = part

    low, front = plan[sources + 1 + 2 * pair], plan[sources + 2 + 2 * pair]
    products(tokens[...], (query_w, key_w, value_w), low, front, store)


def partial_call(kernel, shapes, operands, scratch, tokens, owners):
    vmem = pl.BlockSpec(memory_space=pltpu.VMEM)
    smem = pl.BlockSpec(memory_space=pltpu.SMEM)
    depth = operands[1].shape[1]
    cols = (GROUP + 2) * HEAD_SIZE
    return pl.pallas_call(
        kernel,
        out_shape=[jax.ShapeDtypeStruct(shape, jnp.float32) for shape in shapes],
        in_specs=[vmem if operand.ndim > 1 else smem for operand in operands],
        out_specs=[vmem for _ in shapes],
        scratch_shapes=scratch,
        compiler_params=pltpu.CompilerParams(vmem_limit_bytes=GRANT * 1024 * 1024),
        cost_estimate=pl.CostEstimate(
            flops=int(2 * owners * tokens * depth * cols),
            bytes_accessed=int(2 * (tokens * depth + owners * cols * (depth + 2 * tokens))),
            transcendentals=0,
        ),
    )(*operands)


def split_shards(
    hidden, w_query, key_projection, value_projection, score_head, lengths, prompt_len, reward
):
    rows = hidden.shape[0]
    depth = w_query.shape[1]
    ctx = lax.axis_index("ctx")
    section = lax.axis_index("sec")
    share = lax.axis_index("tp")
    count = 4
    f16, f32 = jnp.float16, jnp.float32

    steps = (2, 3, 1)
    half_rows = rows // 2
    targets = [(ctx + step) % count for step in (*steps, 0)]
    cuts = pl.pallas_call(
        cut_kernel,
        out_shape=[
            jax.ShapeDtypeStruct((half_rows if step == 2 else rows, depth), hidden.dtype)
            for step in (*steps, 0)
        ],
        in_specs=[
            pl.BlockSpec(memory_space=pltpu.SMEM),
            pl.BlockSpec(memory_space=pl.ANY),
        ],
        out_specs=[pl.BlockSpec(memory_space=pltpu.VMEM)] * 4,
        scratch_shapes=[pltpu.SemaphoreType.DMA((4,))],
        compiler_params=pltpu.CompilerParams(vmem_limit_bytes=4 * 1024 * 1024),
    )(jnp.stack([share, *targets]).astype(jnp.int32), hidden)
    mine = cuts[3]
    sent = {}
    for step, piece in zip(steps, cuts):
        pairs = [(i, (i + step) % count) for i in range(count)]
        sent[step] = lax.ppermute(piece, "ctx", pairs)
    weights = (w_query, key_projection, value_projection)
    cols = (GROUP + 2) * HEAD_SIZE
    chip = 2 * rows
    left = ctx < 2
    low = jnp.where(left, 2, 0)
    plan = jnp.stack(
        [*((ctx - step) % count for step in steps), ctx]
        + [low, jnp.where(left, 1, 0), 2 - low, 1 - ctx % 2, share]
    ).astype(jnp.int32)
    (own,) = partial_call(
        lambda *refs: own_kernel(*refs, sources=count),
        [(count, chip, cols)],
        (plan, mine, swapped(mine, "sec", 0), *weights),
        [],
        chip,
        count,
    )

    sent[2], own = lax.optimization_barrier((sent[2], own))
    swap = swapped(sent[2], "tp", 0)
    sent[1], sent[3], swap, own = lax.optimization_barrier((sent[1], sent[3], swap, own))
    pieces, layout = [], []
    for slot, step in enumerate(steps):
        parts = [(sent[step], None)]
        if step == 2:
            parts = [(sent[step], 0), (swap, 1)]
        for part, half in parts:
            pieces += [part, swapped(part, "sec", 0)]
            layout += [(slot * chip, half), (slot * chip + rows, half)]

    def rest(pair):
        return partial_call(
            lambda *refs: rest_kernel(*refs, pair=pair, layout=layout),
            [(2, count * chip, cols)],
            (plan, *pieces, own, *weights),
            [pltpu.VMEM((len(steps) * chip, depth), jnp.bfloat16)],
            len(steps) * chip,
            2,
        )[0]

    first = rest(0)
    second = rest(1)

    def reduced(first, second):
        far = first[0].astype(f16)
        fold = lax.ppermute(far, "ctx", [(0, 1), (3, 2)])
        inner = first[1].astype(f16)
        middle = lax.ppermute(inner, "ctx", [(1, 2), (2, 1)])
        skip = lax.ppermute(inner, "ctx", [(0, 2), (3, 1)])
        folded = (first[0] + fold.astype(f32)).astype(f16)
        ends = lax.ppermute(folded, "ctx", [(1, 3), (2, 0)])
        beside = second[0].astype(f16)
        near = lax.ppermute(beside, "ctx", [(0, 1), (1, 0), (2, 3), (3, 2)])
        total = second[1] + middle.astype(f32) + skip.astype(f32)
        total, near = lax.optimization_barrier((total, near))
        total, ends = lax.optimization_barrier((total + near.astype(f32), ends))
        total = total + ends.astype(f32)
        return (total * (1.0 / LINK_SCALE)).astype(jnp.bfloat16)

    mine = reduced(first, second)
    wide = GROUP * HEAD_SIZE
    smem = pl.BlockSpec(memory_space=pltpu.SMEM)
    where = jnp.stack([section, ctx]).astype(jnp.int32)
    sums = pl.pallas_call(
        lambda plan, *refs: attention_kernel(*refs, rows),
        out_shape=jax.ShapeDtypeStruct((4 * count, 1, 2 * rows), f32),
        grid_spec=pltpu.PrefetchScalarGridSpec(
            num_scalar_prefetch=1,
            grid=(1,),
            in_specs=[
                smem,
                smem,
                pl.BlockSpec(mine.shape, lambda i, plan: (0, 0)),
                pl.BlockSpec((1, wide), lambda i, plan: (0, plan[1])),
            ],
            out_specs=pl.BlockSpec((4 * count, 1, 2 * rows), lambda i, plan: (0, 0, 0)),
        ),
        compiler_params=pltpu.CompilerParams(vmem_limit_bytes=12 * 1024 * 1024),
    )(where, lengths, where, mine, score_head)

    spread = lax.all_to_all(sums, ("ctx", "sec", "tp"), 0, 0, tiled=True)
    vmem = pl.BlockSpec(memory_space=pltpu.VMEM)
    kl_term, objective = pl.pallas_call(
        final_kernel,
        out_shape=[jax.ShapeDtypeStruct((1, rows), f32)] * 2,
        in_specs=[smem, smem, smem, smem, vmem],
        out_specs=[vmem, vmem],
        compiler_params=pltpu.CompilerParams(vmem_limit_bytes=4 * 1024 * 1024),
    )(lengths, prompt_len, reward, where, spread)
    return (kl_term.reshape(rows), objective.reshape(rows))


def solution(mesh):
    placed = (
        P(("grp", "ctx", "sec"), None),
        P("sec", "ctx", "tp"),
        P("sec", "ctx", "tp"),
        P("sec", "ctx", "tp"),
        P("sec", "tp"),
        P("grp"),
        P("grp"),
        P("grp"),
    )
    own_heads = KEY_VALUE_HEADS // mesh.shape["tp"]
    by_heads = mesh.shape["ctx"] == 4 and own_heads == 4
    return jax.shard_map(
        split_shards if by_heads else gathered_shards,
        mesh=mesh,
        in_specs=placed,
        out_specs=(P(("grp", "ctx", "sec")), P(("grp", "ctx", "sec"))),
        check_vma=False,
    )
```
